256 devices in a mesh: expert: 128 (over y, x, z), dp: 2 (over core).
Axes of the slice: x: 4, y: 4, z: 8, core: 2. Of those that a mesh axis runs over, the one named last changes fastest.
Arguments:
- tokens: bfloat16 [32768, 2048], P(('expert', 'dp')), may hold values from -6 to 6
- out_grad: bfloat16 [32768, 2048], P(('expert', 'dp')), may hold values from -6 to 6
- gates: float32 [32768, 8], P(('expert', 'dp')), may hold values from 0.05 to 0.5
- expert_ids: int32 [32768, 8], P(('expert', 'dp')), may hold values from 0 to 127, all different within a row; in each aligned block of 128 rows (0 to 127, 128 to 255, ...) at most 10 rows name the same one
- w_gate: bfloat16 [128, 2048, 384], P('expert', 'dp'), may hold values from -0.125 to 0.125
- w_up: bfloat16 [128, 2048, 384], P('expert', 'dp'), may hold values from -0.125 to 0.125
- w_down: bfloat16 [128, 2048, 384], P('expert', 'dp'), may hold values from -0.3125 to 0.3125
Outputs:
- input_grad: bfloat16 [32768, 2048], P(('expert', 'dp'))
- grad_gate: float32 [128, 2048, 384], P('expert', 'dp')
- grad_up: float32 [128, 2048, 384], P('expert', 'dp')
- grad_down: float32 [128, 2048, 384], P('expert', 'dp')
The draws below stay inside these ranges and needn't reach their ends.
Inputs may be any that keep to these rules, and one draw needn't show every extreme that they name: `expert_ids`: among the 128 tokens of one device no expert is named more than 10 times, and in every draw some device names some expert exactly 10 times. The ids of one token differ.
All inputs are finite; a program needn't handle non-finite values.
Results may differ from the reference program's by a relative error of at most 0.0065.
Values may be sent and summed in bfloat16 or wider, within the bound.
A program may use at most 128 MiB of HBM per device.

```python
import math
import jax
import jax.numpy as jnp
import numpy as np
from jax import lax

D = 2048
FF = 384
TOP = 8
TOK_DEV = 128
EXPERTS = 128
CAP = 10
TOKENS = 32768
N_EXPERT = 128
N_DP = 2


def block_levels(key, shape, pieces, smallest, top_value):
    def one(axis_at, parts):
        heights = jax.random.uniform(jax.random.fold_in(jax.random.fold_in(key, 6), axis_at), (parts,), jnp.float32, smallest / len(pieces), top_value / len(pieces))
        return jnp.repeat(jnp.exp(heights), shape[axis_at] // parts).reshape((-1,) + (1,) * (len(shape) - axis_at - 1))

    level = one(*pieces[0])
    for cut in pieces[1:]:
        level = level * one(*cut)
    return level


def deal_out(own_key, own, number, rows, number_of, top, most, lean):
    ranking = jax.random.permutation(own_key, number_of)
    heavy_load, ordinary = shares(number_of, rows * top, most, lean, True), shares(number_of, rows * top, most, lean, False)
    places = jnp.arange(number_of)

    def named(sizes, rotation):
        used = int((sizes > 0).sum())
        fixed = max(1, used // 4)
        moved = fixed + (places - fixed + rotation * (used - fixed)) % max(1, number_of - fixed)
        return jnp.zeros((number_of,), jnp.int32).at[ranking[jnp.where(places < fixed, places, moved)]].set(jnp.asarray(sizes, jnp.int32))

    sizes = jnp.where(number % 4 == 0, named(heavy_load, number // 4), named(ordinary, number - number // 4 - 1))
    mixed = jax.random.permutation(jax.random.fold_in(own, 3), number_of)
    donor, receiver = mixed[0:number_of // 2 * 2:2], mixed[1:number_of // 2 * 2:2]
    slack = jnp.minimum(sizes[donor] - 1, most - sizes[receiver]) // 2
    slack = jnp.where((donor == ranking[0]) | (receiver == ranking[0]) | (sizes[receiver] == 0), 0, jnp.maximum(slack, 0))
    moved = jax.random.randint(jax.random.fold_in(own, 4), (number_of // 2,), 0, 1 << 20) % (slack + 1)
    sizes = sizes.at[donor].add(-moved).at[receiver].add(moved)
    members = jnp.searchsorted(jnp.cumsum(sizes), jnp.arange(rows * top), side="right").astype(jnp.int32)
    table = members.reshape(top, rows).T
    table = table[jax.random.permutation(jax.random.fold_in(own, 1), rows)]
    rotation = jax.random.randint(jax.random.fold_in(own, 2), (rows, 1), 0, top)
    return jnp.take_along_axis(table, (jnp.arange(top)[None, :] + rotation) % top, axis=1)


def shares(amount, total, bound, lean, full):
    weights = [(1 << 20) // math.isqrt(rank ** lean) + 1 for rank in range(1, amount + 1)]
    largest = bound if full else min(bound, max(-(-total // amount), total * weights[0] // sum(weights)))
    least = 1 if total - largest >= amount - 1 else 0
    holding, spare = [largest] + [least] * (amount - 1), total - largest - least * (amount - 1)
    while spare > 0:
        candidates = [i for i in range(1, amount) if holding[i] < largest] or [i for i in range(1, amount) if holding[i] < bound]
        pool, left = sum([weights[i] for i in candidates]), spare
        for i in candidates:
            addition = min(bound - holding[i], max(1, left * weights[i] // pool), spare)
            holding[i] = holding[i] + addition
            spare = spare - addition
    return np.array(holding)


def scatter_about(rng, dims, deviation, bound, pieces=(), kind=jnp.bfloat16):
    result = jax.random.normal(rng, dims, jnp.float32) * deviation
    if len(pieces) > 0:
        result = block_levels(rng, dims, pieces, -0.22, 0.18) * result
    return jnp.clip(result, min=-bound, max=bound).astype(kind)


def setup_inputs(seed: int = 0) -> dict:
    splits = jax.random.split(jax.random.key(seed), 8)
    tokens = scatter_about(splits[0], (TOKENS, D), 1.0, 6.0, ((0, 256),))
    out_grad = scatter_about(splits[1], (TOKENS, D), 1.0, 6.0, ((0, 256),))
    gates = jnp.clip(jnp.exp(math.log(0.5) - 2.3025851 * jax.random.uniform(splits[2], (TOKENS, TOP), jnp.float32) ** block_levels(splits[2], (TOKENS, TOP), ((0, 256),), -0.2, 0.2)), 0.05, 0.5)
    expert_ids_keys = jax.random.split(jax.random.fold_in(splits[3], 1), TOKENS // TOK_DEV)
    expert_ids_turns = jax.random.permutation(jax.random.fold_in(splits[3], 3), TOKENS // TOK_DEV)
    expert_ids = jax.vmap(lambda own, number: deal_out(jax.random.fold_in(splits[3], 2), own, number, TOK_DEV, EXPERTS, TOP, CAP, 2))(expert_ids_keys, expert_ids_turns).reshape((TOKENS, TOP))
    w_gate = scatter_about(splits[4], (EXPERTS, D, FF), D ** -0.5, 0.125, ((0, 128), (1, 2)))
    w_up = scatter_about(splits[5], (EXPERTS, D, FF), D ** -0.5, 0.125, ((0, 128), (1, 2)))
    w_down = scatter_about(splits[6], (EXPERTS, D, FF), FF ** -0.5, 0.3125, ((0, 128), (1, 2)))
    return dict(tokens=tokens, out_grad=out_grad, gates=gates, expert_ids=expert_ids, w_gate=w_gate, w_up=w_up, w_down=w_down)


def reference(tokens, out_grad, gates, expert_ids, w_gate, w_up, w_down):
    pair_count = TOKENS * TOP
    most_rows = N_EXPERT * N_DP * CAP
    flat_ids = expert_ids.reshape(-1)
    tokens_pad = jnp.concatenate([tokens, jnp.zeros((1, D), tokens.dtype)], axis=0)
    grads_pad = jnp.concatenate([out_grad, jnp.zeros((1, D), out_grad.dtype)], axis=0)
    gates_flat = jnp.concatenate([gates.reshape(-1), jnp.zeros((1,), gates.dtype)], axis=0)

    def one_expert(dx_total, inputs):
        expert, gate_w, up_w, down_w = inputs
        picked = jnp.nonzero(flat_ids == expert, size=most_rows, fill_value=pair_count)[0].astype(jnp.int32)
        tok_index = jnp.where(picked < pair_count, picked // TOP, TOKENS).astype(jnp.int32)
        x_rows = tokens_pad[tok_index]
        dy_rows = (gates_flat[picked][:, None] * grads_pad[tok_index].astype(jnp.float32)).astype(jnp.bfloat16)
        gate_pre = jnp.dot(x_rows, gate_w, preferred_element_type=jnp.float32)
        up_pre = jnp.dot(x_rows, up_w, preferred_element_type=jnp.float32)
        sig_gate = jax.nn.sigmoid(gate_pre)
        active = gate_pre * sig_gate
        hidden = (active * up_pre).astype(jnp.bfloat16)
        hidden_grad = jnp.dot(dy_rows, down_w, preferred_element_type=jnp.float32)
        gate_grad = (hidden_grad * up_pre * sig_gate * (1.0 + gate_pre * (1.0 - sig_gate))).astype(jnp.bfloat16)
        up_grad = (hidden_grad * active).astype(jnp.bfloat16)
        grad_g = jnp.dot(x_rows.T, gate_grad, preferred_element_type=jnp.float32)
        grad_u = jnp.dot(x_rows.T, up_grad, preferred_element_type=jnp.float32)
        grad_d = jnp.dot(dy_rows.T, hidden, preferred_element_type=jnp.float32)
        pair_grad = (jnp.dot(gate_grad, gate_w.T, preferred_element_type=jnp.float32)
                     + jnp.dot(up_grad, up_w.T, preferred_element_type=jnp.float32)).astype(jnp.bfloat16)
        dx_total = dx_total.at[tok_index].add(pair_grad.astype(jnp.float32))
        return dx_total, (grad_g, grad_u, grad_d)

    start_total = jnp.zeros((TOKENS + 1, D), jnp.float32)
    expert_list = jnp.arange(EXPERTS, dtype=jnp.int32)
    dx_total, grads = lax.scan(one_expert, start_total, (expert_list, w_gate, w_up, w_down))
    input_grad = dx_total[:TOKENS].astype(jnp.bfloat16)
    return input_grad, grads[0], grads[1], grads[2]
```

```python
import functools

import jax
import jax.numpy as jnp
from jax import lax
from jax.experimental import pallas as pl
from jax.experimental.pallas import tpu as pltpu
from jax.sharding import PartitionSpec as P

BF16 = jnp.bfloat16
F32 = jnp.float32
ZS = 8
CAP = 10
HALF = 4
BLK = HALF * CAP

GOES_RIGHT = ((0, 1), (1, 3), (3, 5), (5, 7))
GOES_LEFT = ((0, 2), (2, 4), (4, 6), (6, 7))
OFFSET = (0, -1, 1, -2, 2, -3, 3, 4)

contract_rows = (((0,), (0,)), ((), ()))
contract_cols = (((1,), (1,)), ((), ()))


def place():
    me = lax.axis_index("expert")
    return lax.rem(me, ZS), lax.div(me, ZS)


def on_line(line, z):
    return {"expert": line * ZS + lax.rem(z + 2 * ZS, ZS)}


def send(src, dst, sems, device):
    return pltpu.make_async_remote_copy(
        src_ref=src, dst_ref=dst, send_sem=sems[0], recv_sem=sems[1],
        device_id=device, device_id_type=pl.DeviceIdType.MESH,
    )


def meet(lines):
    z, line = place()
    barrier = pltpu.get_barrier_semaphore()

    def greet_line(j, c):
        pl.semaphore_signal(barrier, inc=1, device_id=on_line(line, z + j), device_id_type=pl.DeviceIdType.MESH)
        return c

    def greet_plane(d, c):
        other = lax.rem(line + d, lines)
        pl.semaphore_signal(barrier, inc=1, device_id=on_line(other, z), device_id_type=pl.DeviceIdType.MESH)
        return c

    lax.fori_loop(1, ZS, greet_line, 0)
    lax.fori_loop(1, lines, greet_plane, 0)
    pl.semaphore_wait(barrier, ZS + lines - 2)


def dispatch_kernel(lines, meta_ref, tok_ref, grad_ref, pick_ref, x_out, dy_out,
                    meta, blocks_x, blocks_g, out_x, out_g, gate_col,
                    meta_send, meta_recv, zs_send, zs_recv, pl_send, pl_recv, own_sem):
    z, line = place()
    toks = tok_ref.shape[0]
    width = tok_ref.shape[1]
    rows_half = lines * BLK
    meet(lines)

    def block(ref, p):
        return ref.at[pl.ds(p * toks, toks)]

    sources = (tok_ref, grad_ref)
    gathered = (blocks_x, blocks_g)

    def hop(t, src, dst, right):
        ref = sources[t] if src == 0 else block(gathered[t], src)
        return send(ref, block(gathered[t], dst), (zs_send.at[t, dst], zs_recv.at[t, dst]), on_line(line, z + 1 if right else z - 1))

    own = [pltpu.make_async_copy(sources[t], block(gathered[t], 0), own_sem.at[t]) for t in (0, 1)]
    metas = [send(meta_ref, meta.at[p], (meta_send.at[p], meta_recv.at[p]), on_line(line, z - OFFSET[p])) for p in range(1, ZS)]
    for m in metas:
        m.start()
    r1 = [hop(t, 0, 1, True) for t in (0, 1)]
    l1 = [hop(t, 0, 2, False) for t in (0, 1)]
    for t in (0, 1):
        r1[t].start()
        l1[t].start()
        own[t].start()
    meta[0] = meta_ref[...]
    for m in metas:
        m.wait()

    before = (lax.broadcasted_iota(jnp.int32, (toks, toks), 0) < lax.broadcasted_iota(jnp.int32, (toks, toks), 1)).astype(F32).astype(BF16)
    expert = (lax.broadcasted_iota(jnp.int32, (lines, toks), 0) * ZS + z).astype(F32)
    slot = lax.broadcasted_iota(jnp.int32, (rows_half, 1), 0).astype(F32)
    slot_line = jnp.floor((slot + 0.5) / BLK)
    slot_in = slot - slot_line * BLK
    spread = (slot_line == lax.broadcasted_iota(jnp.int32, (rows_half, lines), 1).astype(F32)).astype(F32).astype(BF16)
    spread3 = jnp.concatenate([spread, spread, spread], axis=1)
    for h in (0, 1):
        places, weights = [], []
        for s in range(HALF):
            m = meta[h * HALF + s]
            named = jnp.zeros((lines, toks), F32)
            weight = jnp.zeros((lines, toks), F32)
            for k in range(8):
                hit = m[k : k + 1, :] == expert
                named = named + jnp.where(hit, 1.0, 0.0)
                weight = weight + jnp.where(hit, m[8 + k : 9 + k, :], 0.0)
            rank = jnp.dot(named.astype(BF16), before, preferred_element_type=F32)
            places.append(jnp.where(named > 0, rank + s * CAP, -1.0))
            weights.append(weight)
        placed = jnp.dot(spread, jnp.concatenate(places, axis=1).astype(BF16), preferred_element_type=F32)
        pick = placed == slot_in
        pick_ref[h] = jnp.where(pick, 1.0, 0.0).astype(BF16)
        weight = jnp.concatenate(weights, axis=1)
        high = weight.astype(BF16)
        rest = weight - high.astype(F32)
        mid = rest.astype(BF16)
        low = (rest - mid.astype(F32)).astype(BF16)
        spread_w = jnp.dot(spread3, jnp.concatenate([high, mid, low], axis=0), preferred_element_type=F32)
        gate_col[h] = jnp.sum(jnp.where(pick, spread_w, 0.0), axis=1, keepdims=True)

    groups = 4
    rows = rows_half // groups
    send_bufs = (out_x, out_g)
    results = (x_out, dy_out)

    def plane_send(t, h, d):
        other = lax.rem(line + d, lines)
        return send(send_bufs[t].at[h, other], results[t].at[h, line], (pl_send.at[t, h, d], pl_recv.at[t, h, d]), on_line(other, z))

    def own_rows(t, h):
        return pltpu.make_async_copy(send_bufs[t].at[h, line], results[t].at[h, line], pl_send.at[t, h, 0])

    def route(t, h):
        def part(g, c):
            at = pl.ds(pl.multiple_of(g * rows, rows), rows)
            picked = jnp.dot(
                pick_ref[h, at, :],
                gathered[t][pl.ds(h * HALF * toks, HALF * toks), :],
                preferred_element_type=F32,
            )
            if t == 1:
                picked = picked * gate_col[h, at, :]
            per = lines // groups
            send_bufs[t][h, pl.ds(g * per, per)] = picked.reshape(per, BLK // 8, 8, width).astype(BF16)
            return c

        lax.fori_loop(0, groups, part, 0)

        def go(d, c):
            plane_send(t, h, d).start()
            return c

        lax.fori_loop(1, lines, go, 0)
        own_rows(t, h).start()

    for t in (0, 1):
        own[t].wait()
    r2, l2 = [], []
    for t in (0, 1):
        r1[t].wait()
        r2.append(hop(t, 1, 3, True))
        r2[t].start()
        l1[t].wait()
        l2.append(hop(t, 2, 4, False))
        l2[t].start()
    r3, l3 = [], []
    for t in (0, 1):
        r2[t].wait()
        r3.append(hop(t, 3, 5, True))
        r3[t].start()
        l2[t].wait()
        l3.append(hop(t, 4, 6, False))
        l3[t].start()
    route(0, 0)
    route(1, 0)
    r3[0].wait()
    r4 = hop(0, 5, 7, True)
    r4.start()
    l3[0].wait()
    r3[1].wait()
    l3[1].wait()
    l4 = hop(1, 6, 7, False)
    l4.start()
    r4.wait()
    route(0, 1)
    l4.wait()
    route(1, 1)

    for h in (0, 1):
        for t in (0, 1):
            own_rows(t, h).wait()

            def land(d, c, t=t, h=h):
                plane_send(t, h, d).wait()
                return c

            lax.fori_loop(1, lines, land, 0)


def dispatch(meta, tokens, out_grad, lines):
    toks, width = tokens.shape
    rows_half = lines * BLK
    any_spec = pl.BlockSpec(memory_space=pl.ANY)
    vmem = pl.BlockSpec(memory_space=pltpu.VMEM)
    slots = jax.ShapeDtypeStruct((2, lines, BLK // 8, 8, width), BF16)
    return pl.pallas_call(
        functools.partial(dispatch_kernel, lines),
        out_shape=(jax.ShapeDtypeStruct((2, rows_half, HALF * toks), BF16), slots, slots),
        in_specs=[vmem, any_spec, any_spec],
        out_specs=(vmem, any_spec, any_spec),
        scratch_shapes=[
            pltpu.VMEM((ZS, 16, toks), F32),
            pltpu.VMEM((ZS * toks, width), BF16),
            pltpu.VMEM((ZS * toks, width), BF16),
            pltpu.VMEM((2, lines, BLK // 8, 8, width), BF16),
            pltpu.VMEM((2, lines, BLK // 8, 8, width), BF16),
            pltpu.VMEM((2, rows_half, 1), F32),
            pltpu.SemaphoreType.DMA((ZS,)),
            pltpu.SemaphoreType.DMA((ZS,)),
            pltpu.SemaphoreType.DMA((2, ZS)),
            pltpu.SemaphoreType.DMA((2, ZS)),
            pltpu.SemaphoreType.DMA((2, 2, lines)),
            pltpu.SemaphoreType.DMA((2, 2, lines)),
            pltpu.SemaphoreType.DMA((2,)),
        ],
        compiler_params=pltpu.CompilerParams(
            collective_id=0, has_side_effects=True, vmem_limit_bytes=48 << 20
        ),
        name="dispatch",
    )(meta, tokens, out_grad)


def combine_kernel(lines, pick_ref, rows_ref, out_ref, back, part, buf, stage,
                   pl_send, pl_recv, zs_send, zs_recv):
    z, line = place()
    toks, width = out_ref.shape
    meet(lines)

    def plane_send(h, d):
        other = lax.rem(line + d, lines)
        return send(rows_ref.at[h, other], back.at[h, line], (pl_send.at[h, d], pl_recv.at[h, d]), on_line(other, z))

    def own_rows(h):
        return pltpu.make_async_copy(rows_ref.at[h, line], back.at[h, line], pl_send.at[h, 0])

    for h in (1, 0):
        own_rows(h).start()

        def go(d, c, h=h):
            plane_send(h, d).start()
            return c

        lax.fori_loop(1, lines, go, 0)

    def gather(h):
        own_rows(h).wait()

        def land(d, c):
            plane_send(h, d).wait()
            return c

        lax.fori_loop(1, lines, land, 0)
        returned = back[h].reshape(lines * BLK, width)
        for s in range(HALF):
            part[h * HALF + s] = lax.dot_general(
                pick_ref[h, :, s * toks : (s + 1) * toks], returned, contract_rows,
                preferred_element_type=F32,
            )

    def hop(dst, right):
        return send(stage.at[dst], buf.at[dst], (zs_send.at[dst], zs_recv.at[dst]), on_line(line, z + 1 if right else z - 1))

    half = width // 2
    gather(1)
    stage[7, :, :half] = part[7, :, :half].astype(BF16)
    stage[7, :, half:] = part[7, :, half:].astype(BF16)
    r4 = send(stage.at[7, :, pl.ds(0, half)], buf.at[6, :, pl.ds(0, half)], (zs_send.at[6], zs_recv.at[6]), on_line(line, z + 1))
    l4 = send(stage.at[7, :, pl.ds(half, half)], buf.at[5, :, pl.ds(half, half)], (zs_send.at[5], zs_recv.at[5]), on_line(line, z - 1))
    r4.start()
    l4.start()

    def forward(p):
        stage[p] = (part[p] + buf[p].astype(F32)).astype(BF16)

    r4.wait()
    stage[6, :, :half] = (part[6, :, :half] + buf[6, :, :half].astype(F32)).astype(BF16)
    stage[6, :, half:] = part[6, :, half:].astype(BF16)
    r3 = send(stage.at[6], buf.at[4], (zs_send.at[4], zs_recv.at[4]), on_line(line, z + 1))
    r3.start()
    l4.wait()
    stage[5, :, :half] = part[5, :, :half].astype(BF16)
    stage[5, :, half:] = (part[5, :, half:] + buf[5, :, half:].astype(F32)).astype(BF16)
    l3 = send(stage.at[5], buf.at[3], (zs_send.at[3], zs_recv.at[3]), on_line(line, z - 1))
    l3.start()
    r3.wait()
    forward(4)
    r2 = send(stage.at[4], buf.at[2], (zs_send.at[2], zs_recv.at[2]), on_line(line, z + 1))
    r2.start()
    gather(0)
    l3.wait()
    forward(3)
    l2 = send(stage.at[3], buf.at[1], (zs_send.at[1], zs_recv.at[1]), on_line(line, z - 1))
    l2.start()
    r2.wait()
    forward(2)
    r1 = send(stage.at[2], buf.at[0], (zs_send.at[0], zs_recv.at[0]), on_line(line, z + 1))
    r1.start()
    l2.wait()
    forward(1)
    l1 = send(stage.at[1], buf.at[7], (zs_send.at[7], zs_recv.at[7]), on_line(line, z - 1))
    l1.start()
    r1.wait()
    l1.wait()
    out_ref[...] = (part[0] + buf[0].astype(F32) + buf[7].astype(F32)).astype(BF16)


def combine(pick, rows, lines, toks):
    width = rows.shape[-1]
    vmem = pl.BlockSpec(memory_space=pltpu.VMEM)
    return pl.pallas_call(
        functools.partial(combine_kernel, lines),
        out_shape=jax.ShapeDtypeStruct((toks, width), BF16),
        in_specs=[vmem, pl.BlockSpec(memory_space=pl.ANY)],
        out_specs=vmem,
        scratch_shapes=[
            pltpu.VMEM((2, lines, BLK // 8, 8, width), BF16),
            pltpu.VMEM((ZS, toks, width), F32),
            pltpu.VMEM((ZS, toks, width), BF16),
            pltpu.VMEM((ZS, toks, width), BF16),
            pltpu.SemaphoreType.DMA((2, lines)),
            pltpu.SemaphoreType.DMA((2, lines)),
            pltpu.SemaphoreType.DMA((ZS,)),
            pltpu.SemaphoreType.DMA((ZS,)),
        ],
        compiler_params=pltpu.CompilerParams(
            collective_id=1, has_side_effects=True, vmem_limit_bytes=48 << 20
        ),
        name="combine",
    )(pick, rows)


def local(tokens, out_grad, gates, expert_ids, w_gate, w_up, w_down):
    lines = lax.axis_size("expert") // ZS
    toks, width = tokens.shape
    meta = jnp.concatenate([expert_ids.astype(F32).T, gates.T], axis=0)
    pick, x_slots, dy_slots = dispatch(meta, tokens, out_grad, lines)
    slot_count = 2 * lines * BLK
    x_rows = x_slots.reshape(slot_count, width)
    dy_rows = dy_slots.reshape(slot_count, width)
    gate_w = lax.all_gather(w_gate[0], "dp", axis=0, tiled=True)
    up_w = lax.all_gather(w_up[0], "dp", axis=0, tiled=True)
    down_w = lax.all_gather(w_down[0], "dp", axis=0, tiled=True)

    gate_pre = jnp.dot(x_rows, gate_w, preferred_element_type=F32)
    up_pre = jnp.dot(x_rows, up_w, preferred_element_type=F32)
    sig = jax.nn.sigmoid(gate_pre)
    active = gate_pre * sig
    hidden = (active * up_pre).astype(BF16)
    hidden_grad = jnp.dot(dy_rows, down_w, preferred_element_type=F32)
    gate_grad = (hidden_grad * up_pre * sig * (1.0 + gate_pre * (1.0 - sig))).astype(BF16)
    up_grad = (hidden_grad * active).astype(BF16)
    row_out = (
        lax.dot_general(gate_grad, gate_w, contract_cols, preferred_element_type=F32)
        + lax.dot_general(up_grad, up_w, contract_cols, preferred_element_type=F32)
    ).astype(BF16)

    def weight_grad(rows, grads):
        full = lax.dot_general(rows, grads, contract_rows, preferred_element_type=F32)
        return lax.psum_scatter(full, "dp", scatter_dimension=0, tiled=True)[None]

    grad_gate = weight_grad(x_rows, gate_grad)
    grad_up = weight_grad(x_rows, up_grad)
    grad_down = weight_grad(dy_rows, hidden)
    input_grad = combine(pick, row_out.reshape(x_slots.shape), lines, toks)
    return input_grad, grad_gate, grad_up, grad_down


def solution(mesh):
    rows = P(("expert", "dp"), None)
    weights = P("expert", "dp", None)
    return jax.shard_map(
        local,
        mesh=mesh,
        in_specs=(rows, rows, rows, rows, weights, weights, weights),
        out_specs=(rows, weights, weights, weights),
        check_vma=False,
    )
```

```python
import functools

import jax
import jax.numpy as jnp
from jax import lax
from jax.experimental import pallas as pl
from jax.experimental.pallas import tpu as pltpu
from jax.sharding import PartitionSpec as P

BF16 = jnp.bfloat16
F32 = jnp.float32
MESH = pl.DeviceIdType.MESH
ZS = 8
SUB = 8
GROUP = 4

OFFSET = (0, -1, 1, -2, 2, -3, 3, 4)
MAIN = (0, 1, 2, 3, 4, 6, 7, 8)
OVER = (5, 9)
CHUNKS = 10
SLOTS_OUT = 5

contract_rows = (((0,), (0,)), ((), ()))
contract_cols = (((1,), (1,)), ((), ()))


def kernel(lines, meta_ref, tok_ref, grad_ref, wg_ref, wu_ref, wd_ref,
           out_ref, gg_ref, gu_ref, gd_ref,
           meta, block_x, block_g, out_x, out_g, in_x, in_g, weights, acc, other_acc,
           pick_main, pick_over, gate_col, back, stage, buf,
           meta_send, meta_recv, zs_send, zs_recv, pl_send, pl_recv, rt_send, rt_recv,
           w_send, w_recv, a_send, a_recv, rs_send, rs_recv, own_sem):
    me = lax.axis_index("expert")
    core = lax.axis_index("dp")
    z, line = lax.rem(me, ZS), lax.div(me, ZS)
    toks, width = tok_ref.shape
    depth = wg_ref.shape[1]
    rows = lines * SUB
    half = width // 2

    def along_z(j):
        return {"expert": line * ZS + lax.rem(z + j + 2 * ZS, ZS)}

    def in_plane(other):
        return {"expert": other * ZS + z}

    sibling = {"dp": 1 - core}

    def send(src, dst, send_sem, recv_sem, device):
        return pltpu.make_async_remote_copy(
            src_ref=src, dst_ref=dst, send_sem=send_sem, recv_sem=recv_sem,
            device_id=device, device_id_type=MESH,
        )

    barrier = pltpu.get_barrier_semaphore()

    def greet_line(j, c):
        pl.semaphore_signal(barrier, inc=1, device_id=along_z(j), device_id_type=MESH)
        return c

    def greet_plane(d, c):
        pl.semaphore_signal(barrier, inc=1, device_id=in_plane(lax.rem(line + d, lines)), device_id_type=MESH)
        return c

    lax.fori_loop(1, ZS, greet_line, 0)
    lax.fori_loop(1, lines, greet_plane, 0)
    pl.semaphore_signal(barrier, inc=1, device_id=sibling, device_id_type=MESH)
    pl.semaphore_wait(barrier, ZS + lines - 1)

    sources = (tok_ref, grad_ref)
    gathered = (block_x, block_g)
    send_bufs = (out_x, out_g)
    recv_bufs = (in_x, in_g)

    def hop(t, src, dst, j):
        ref = sources[t] if src == 0 else gathered[t].at[src]
        return send(ref, gathered[t].at[dst], zs_send.at[t, dst], zs_recv.at[t, dst], along_z(j))

    own = [pltpu.make_async_copy(sources[t], gathered[t].at[0], own_sem.at[t]) for t in (0, 1)]
    metas = [send(meta_ref, meta.at[p], meta_send.at[p], meta_recv.at[p], along_z(-OFFSET[p])) for p in range(1, ZS)]
    for t in (0, 1):
        own[t].start()
        hop(t, 0, 1, 1).start()
        hop(t, 0, 2, -1).start()
    for m in metas:
        m.start()

    w_refs = (wg_ref, wu_ref, wd_ref)

    def mine(i):
        return weights.at[i, pl.ds(pl.multiple_of(core * depth, depth), depth)]

    w_remote = [send(w_refs[i].at[0], mine(i), w_send.at[i], w_recv.at[i], sibling) for i in range(3)]
    w_local = [pltpu.make_async_copy(w_refs[i].at[0], mine(i), own_sem.at[2 + i]) for i in range(3)]
    for i in range(3):
        w_remote[i].start()
        w_local[i].start()

    def iota(shape, axis):
        return lax.broadcasted_iota(jnp.int32, shape, axis)

    def ones_where(mask):
        return jnp.where(mask, 1.0, 0.0).astype(BF16)

    def prepare(p, c):
        m = meta[p]
        expert = (iota((lines, toks), 0) * ZS + z).astype(F32)
        named = jnp.zeros((lines, toks), F32)
        weight = jnp.zeros((lines, toks), F32)
        for k in range(8):
            hit = m[k : k + 1, :] == expert
            named = named + jnp.where(hit, 1.0, 0.0)
            weight = weight + jnp.where(hit, m[8 + k : 9 + k, :], 0.0)
        before = ones_where(iota((toks, toks), 0) < iota((toks, toks), 1))
        rank = jnp.dot(named.astype(BF16), before, preferred_element_type=F32)
        taken = named > 0
        shift = (lax.rem(p, GROUP) * 2).astype(F32) - SUB
        in_main = jnp.where(taken & (rank < SUB), rank, -1.0)
        in_over = jnp.where(taken & (rank >= SUB), rank + shift, -1.0)
        row = iota((rows, 1), 0)
        spread = ones_where(lax.div(row, SUB) == iota((rows, lines), 1))
        within = lax.rem(row, SUB).astype(F32)
        placed = jnp.dot(spread, jnp.concatenate([in_main, in_over], axis=1).astype(BF16), preferred_element_type=F32)
        main, over = placed[:, :toks] == within, placed[:, toks:] == within
        high = weight.astype(BF16)
        rest = weight - high.astype(F32)
        mid = rest.astype(BF16)
        low = (rest - mid.astype(F32)).astype(BF16)
        spread_w = jnp.dot(
            jnp.concatenate([spread, spread, spread], axis=1),
            jnp.concatenate([high, mid, low], axis=0),
            preferred_element_type=F32,
        )
        pick_main[p] = ones_where(main)
        pick_over[p] = ones_where(over)
        gate_col[p] = jnp.sum(jnp.where(main, spread_w, 0.0), axis=1, keepdims=True)
        at = ZS + lax.div(p, GROUP)
        gate_col[at] = gate_col[at] + jnp.sum(jnp.where(over, spread_w, 0.0), axis=1, keepdims=True)
        return c

    def chunk_send(t, k, d):
        other = lax.rem(line + d, lines)
        return send(send_bufs[t].at[k % SLOTS_OUT, other], recv_bufs[t].at[k, line], pl_send.at[t, k], pl_recv.at[t, k], in_plane(other))

    def sent(t, k):
        rest = send_bufs[t].at[k % SLOTS_OUT, pl.ds(0, lines - 1)]
        return pltpu.make_async_copy(rest, rest, pl_send.at[t, k])

    def route(k, places):
        for t in (0, 1):
            if k >= SLOTS_OUT:
                sent(t, k - SLOTS_OUT).wait()
            picks = pick_main if len(places) == 1 else pick_over
            total = None
            for p in places:
                part = jnp.dot(picks[p], gathered[t][p], preferred_element_type=F32)
                total = part if total is None else total + part
            if t == 1:
                total = total * gate_col[places[0] if len(places) == 1 else ZS + places[0] // GROUP]
            send_bufs[t][k % SLOTS_OUT] = total.reshape(lines, SUB, width).astype(BF16)

            def go(d, c, t=t):
                chunk_send(t, k, d).start()
                return c

            lax.fori_loop(1, lines, go, 0)
            pltpu.make_async_copy(send_bufs[t].at[k % SLOTS_OUT, line], recv_bufs[t].at[k, line], pl_recv.at[t, k]).start()

    def arrived(ref, sem):
        pltpu.make_async_copy(ref, ref, sem).wait()

    def expert(k):
        for t in (0, 1):
            arrived(recv_bufs[t].at[k], pl_recv.at[t, k])
        x = in_x[k].reshape(rows, width)
        dy = in_g[k].reshape(rows, width)
        gate_pre = jnp.dot(x, weights[0], preferred_element_type=F32)
        up_pre = jnp.dot(x, weights[1], preferred_element_type=F32)
        hidden_grad = jnp.dot(dy, weights[2], preferred_element_type=F32)
        sig = jax.nn.sigmoid(gate_pre)
        active = gate_pre * sig
        hidden = (active * up_pre).astype(BF16)
        gate_grad = (hidden_grad * up_pre * sig * (1.0 + gate_pre * (1.0 - sig))).astype(BF16)
        up_grad = (hidden_grad * active).astype(BF16)
        acc[0] += lax.dot_general(x, gate_grad, contract_rows, preferred_element_type=F32)
        acc[1] += lax.dot_general(x, up_grad, contract_rows, preferred_element_type=F32)
        acc[2] += lax.dot_general(dy, hidden, contract_rows, preferred_element_type=F32)
        row_grad = lax.dot_general(
            gate_grad, weights[0], contract_cols, preferred_element_type=F32
        ) + lax.dot_general(up_grad, weights[1], contract_cols, preferred_element_type=F32)
        in_x[k] = row_grad.reshape(lines, SUB, width).astype(BF16)

    def give_back(k):
        def go(d, c):
            other = lax.rem(line + d, lines)
            send(in_x.at[k, other], back.at[k, line], rt_send.at[k], rt_recv.at[k], in_plane(other)).start()
            return c

        lax.fori_loop(1, lines, go, 0)
        pltpu.make_async_copy(in_x.at[k, line], back.at[k, line], rt_recv.at[k]).start()

    gate_col[...] = jnp.zeros_like(gate_col)
    acc[...] = jnp.zeros_like(acc)
    meta[0] = meta_ref[...]
    prepare(0, 0)
    for t in (0, 1):
        own[t].wait()
    route(0, (0,))
    for m in metas:
        m.wait()
    lax.fori_loop(1, ZS, prepare, 0)

    def pass_on(t, src, dst, came, j):
        hop(t, came, src, j).wait()
        hop(t, src, dst, j).start()

    def work(k, c):
        @pl.when(k == 0)
        def _():
            for t in (0, 1):
                pass_on(t, 1, 3, 0, 1)
                pass_on(t, 2, 4, 0, -1)
            route(1, (1,))
            route(2, (2,))
            for i in range(3):
                w_local[i].wait()
                w_remote[i].wait()

        @pl.when(k == 1)
        def _():
            for t in (0, 1):
                pass_on(t, 3, 5, 1, 1)
                pass_on(t, 4, 6, 2, -1)
            route(3, (3,))
            route(4, (4,))
            route(5, (0, 1, 2, 3))

        @pl.when(k == 3)
        def _():
            pass_on(0, 5, 7, 3, 1)
            hop(0, 4, 6, -1).wait()
            hop(1, 3, 5, 1).wait()
            pass_on(1, 6, 7, 4, -1)
            route(6, (5,))
            route(7, (6,))

        @pl.when(k == 5)
        def _():
            hop(0, 5, 7, 1).wait()
            hop(1, 6, 7, -1).wait()
            route(8, (7,))
            route(9, (4, 5, 6, 7))

        expert(k)

        @pl.when((k == 4) | (k >= 6))
        def _():
            give_back(k)

        return c

    lax.fori_loop(0, CHUNKS, work, 0)
    for k in (5, 3, 2, 1, 0):
        give_back(k)

    def acc_rows(i, c):
        return acc.at[i, pl.ds(pl.multiple_of(c * depth, depth), depth)]

    acc_sends = [send(acc_rows(i, 1 - core), other_acc.at[i], a_send.at[i], a_recv.at[i], sibling) for i in range(3)]
    for s in acc_sends:
        s.start()

    def summed(p):
        return lax.dot_general(
            pick_main[p], back[MAIN[p]].reshape(rows, width), contract_rows, preferred_element_type=F32
        ) + lax.dot_general(
            pick_over[p], back[OVER[p // GROUP]].reshape(rows, width), contract_rows, preferred_element_type=F32
        )

    def returned(k):
        arrived(back.at[k], rt_recv.at[k])

    def ring(p, dst, j):
        return send(stage.at[p], buf.at[dst], rs_send.at[dst], rs_recv.at[dst], along_z(j))

    low, high = pl.ds(0, half), pl.ds(half, half)
    returned(9)
    returned(8)
    part = summed(7)
    stage[7] = part.astype(BF16)
    r4 = send(stage.at[7, :, low], buf.at[6, :, low], rs_send.at[6], rs_recv.at[6], along_z(1))
    l4 = send(stage.at[7, :, high], buf.at[5, :, high], rs_send.at[5], rs_recv.at[5], along_z(-1))
    r4.start()
    l4.start()
    returned(7)
    part = summed(6)
    r4.wait()
    stage[6, :, :half] = (part[:, :half] + buf[6, :, :half].astype(F32)).astype(BF16)
    stage[6, :, half:] = part[:, half:].astype(BF16)
    r3 = ring(6, 4, 1)
    r3.start()
    returned(6)
    part = summed(5)
    l4.wait()
    stage[5, :, :half] = part[:, :half].astype(BF16)
    stage[5, :, half:] = (part[:, half:] + buf[5, :, half:].astype(F32)).astype(BF16)
    l3 = ring(5, 3, -1)
    l3.start()

    outs = (gg_ref, gu_ref, gd_ref)
    stores = []
    for i in range(3):
        acc_sends[i].wait()
        other_acc[i] = other_acc[i] + acc[i, pl.ds(pl.multiple_of(core * depth, depth), depth), :]
        stores.append(pltpu.make_async_copy(other_acc.at[i], outs[i].at[0], own_sem.at[i]))
        stores[i].start()

    def forward(p, came):
        part = summed(p)
        came.wait()
        stage[p] = (part + buf[p].astype(F32)).astype(BF16)

    returned(4)
    forward(4, r3)
    r2 = ring(4, 2, 1)
    r2.start()
    returned(5)
    returned(3)
    forward(3, l3)
    l2 = ring(3, 1, -1)
    l2.start()
    returned(2)
    forward(2, r2)
    r1 = ring(2, 0, 1)
    r1.start()
    returned(1)
    forward(1, l2)
    l1 = ring(1, 7, -1)
    l1.start()
    returned(0)
    part = summed(0)
    r1.wait()
    l1.wait()
    out_ref[...] = (part + buf[0].astype(F32) + buf[7].astype(F32)).astype(BF16)

    for k in range(CHUNKS - SLOTS_OUT, CHUNKS):
        for t in (0, 1):
            sent(t, k).wait()
    for k in range(CHUNKS):
        rest = in_x.at[k, pl.ds(0, lines - 1)]
        arrived(rest, rt_send.at[k])
    for s in stores:
        s.wait()


def local(tokens, out_grad, gates, expert_ids, w_gate, w_up, w_down):
    lines = lax.axis_size("expert") // ZS
    toks, width = tokens.shape
    depth, ff = w_gate.shape[1:]
    rows = lines * SUB
    meta = jnp.concatenate([expert_ids.astype(F32).T, gates.T], axis=0)
    any_spec = pl.BlockSpec(memory_space=pl.ANY)
    vmem = pl.BlockSpec(memory_space=pltpu.VMEM)
    dma = pltpu.SemaphoreType.DMA
    grads = jax.ShapeDtypeStruct((1, depth, ff), F32)
    return pl.pallas_call(
        functools.partial(kernel, lines),
        out_shape=(jax.ShapeDtypeStruct((toks, width), BF16), grads, grads, grads),
        in_specs=[vmem] + [any_spec] * 5,
        out_specs=(vmem, any_spec, any_spec, any_spec),
        scratch_shapes=[
            pltpu.VMEM((ZS, 16, toks), F32),
            pltpu.VMEM((ZS, toks, width), BF16),
            pltpu.VMEM((ZS, toks, width), BF16),
            pltpu.VMEM((SLOTS_OUT, lines, SUB, width), BF16),
            pltpu.VMEM((SLOTS_OUT, lines, SUB, width), BF16),
            pltpu.VMEM((CHUNKS, lines, SUB, width), BF16),
            pltpu.VMEM((CHUNKS, lines, SUB, width), BF16),
            pltpu.VMEM((3, 2 * depth, ff), BF16),
            pltpu.VMEM((3, 2 * depth, ff), F32),
            pltpu.VMEM((3, depth, ff), F32),
            pltpu.VMEM((ZS, rows, toks), BF16),
            pltpu.VMEM((ZS, rows, toks), BF16),
            pltpu.VMEM((CHUNKS, rows, 1), F32),
            pltpu.VMEM((CHUNKS, lines, SUB, width), BF16),
            pltpu.VMEM((ZS, toks, width), BF16),
            pltpu.VMEM((ZS, toks, width), BF16),
            dma((ZS,)),
            dma((ZS,)),
            dma((2, ZS)),
            dma((2, ZS)),
            dma((2, CHUNKS)),
            dma((2, CHUNKS)),
            dma((CHUNKS,)),
            dma((CHUNKS,)),
            dma((3,)),
            dma((3,)),
            dma((3,)),
            dma((3,)),
            dma((ZS,)),
            dma((ZS,)),
            dma((5,)),
        ],
        compiler_params=pltpu.CompilerParams(
            collective_id=0, has_side_effects=True, vmem_limit_bytes=61 << 20
        ),
        name="experts_backward",
    )(meta, tokens, out_grad, w_gate, w_up, w_down)


def solution(mesh):
    rows = P(("expert", "dp"), None)
    weights = P("expert", "dp", None)
    return jax.shard_map(
        local,
        mesh=mesh,
        in_specs=(rows, rows, rows, rows, weights, weights, weights),
        out_specs=(rows, weights, weights, weights),
        check_vma=False,
    )
```

```python
import functools

import jax
import jax.numpy as jnp
from jax import lax
from jax.experimental import pallas as pl
from jax.experimental.pallas import tpu as pltpu
from jax.sharding import PartitionSpec as P

BF16 = jnp.bfloat16
F32 = jnp.float32
MESH = pl.DeviceIdType.MESH
ZS = 8
SUB = 8
GROUP = 4

OFFSET = (0, -1, 1, -2, 2, -3, 3, 4)
MAIN = (0, 1, 2, 3, 4, 6, 7, 8)
OVER = (5, 9)
CHUNKS = 10
SLOTS_OUT = 6

contract_rows = (((0,), (0,)), ((), ()))
contract_cols = (((1,), (1,)), ((), ()))


def kernel(lines, ids_ref, gates_ref, tok_ref, grad_ref, wg_ref, wu_ref, wd_ref,
           out_ref, gg_ref, gu_ref, gd_ref,
           meta, block_x, block_g, out_x, out_g, in_x, in_g, weights, acc, other_acc,
           pick_main, pick_over, gate_col, back, stage, buf,
           meta_send, meta_recv, zs_send, zs_recv, pl_send, pl_recv, rt_send, rt_recv,
           w_send, w_recv, a_send, a_recv, rs_send, rs_recv, own_sem):
    me = lax.axis_index("expert")
    core = lax.axis_index("dp")
    z, line = lax.rem(me, ZS), lax.div(me, ZS)
    toks, width = tok_ref.shape
    depth = wg_ref.shape[1]
    rows = lines * SUB
    half = width // 2

    def along_z(j):
        return {"expert": line * ZS + lax.rem(z + j + 2 * ZS, ZS)}

    def in_plane(other):
        return {"expert": other * ZS + z}

    sibling = {"dp": 1 - core}

    def send(src, dst, send_sem, recv_sem, device):
        return pltpu.make_async_remote_copy(
            src_ref=src, dst_ref=dst, send_sem=send_sem, recv_sem=recv_sem,
            device_id=device, device_id_type=MESH,
        )

    barrier = pltpu.get_barrier_semaphore()

    def greet_line(j, c):
        pl.semaphore_signal(barrier, inc=1, device_id=along_z(j), device_id_type=MESH)
        return c

    def greet_plane(d, c):
        pl.semaphore_signal(barrier, inc=1, device_id=in_plane(lax.rem(line + d, lines)), device_id_type=MESH)
        return c

    lax.fori_loop(1, ZS, greet_line, 0)
    lax.fori_loop(1, lines, greet_plane, 0)
    pl.semaphore_signal(barrier, inc=1, device_id=sibling, device_id_type=MESH)
    pl.semaphore_wait(barrier, ZS + lines - 1)

    sources = (tok_ref, grad_ref)
    gathered = (block_x, block_g)
    send_bufs = (out_x, out_g)
    recv_bufs = (in_x, in_g)

    def hop(t, src, dst, j):
        ref = sources[t] if src == 0 else gathered[t].at[src]
        return send(ref, gathered[t].at[dst], zs_send.at[t, dst], zs_recv.at[t, dst], along_z(j))

    def both_ways(t, right, left):
        for (src, dst), j in ((right, 1), (left, -1)):
            hop(t, src, dst, j).start()

    def landed(t, right, left):
        for (src, dst), j in ((right, 1), (left, -1)):
            hop(t, src, dst, j).wait_recv()

    own = [pltpu.make_async_copy(sources[t], gathered[t].at[0], own_sem.at[t]) for t in (0, 1)]
    metas = [send(meta.at[0], meta.at[p], meta_send.at[p], meta_recv.at[p], along_z(-OFFSET[p])) for p in range(1, ZS)]
    meta[0, :8] = ids_ref[...].astype(F32)
    meta[0, 8:] = gates_ref[...]
    for m in metas:
        m.start()
    both_ways(0, (0, 1), (0, 2))
    for t in (0, 1):
        own[t].start()

    w_refs = (wg_ref, wu_ref, wd_ref)

    def mine(i):
        return weights.at[i, pl.ds(pl.multiple_of(core * depth, depth), depth)]

    w_remote = [send(w_refs[i].at[0], mine(i), w_send.at[i], w_recv.at[i], sibling) for i in range(3)]
    w_local = [pltpu.make_async_copy(w_refs[i].at[0], mine(i), own_sem.at[2 + i]) for i in range(3)]
    for i in range(3):
        w_remote[i].start()
        w_local[i].start()

    def iota(shape, axis):
        return lax.broadcasted_iota(jnp.int32, shape, axis)

    def ones_where(mask):
        return jnp.where(mask, 1.0, 0.0).astype(BF16)

    def prepare(p, c):
        m = meta[p]
        expert = (iota((lines, toks), 0) * ZS + z).astype(F32)
        named = jnp.zeros((lines, toks), F32)
        weight = jnp.zeros((lines, toks), F32)
        for k in range(8):
            hit = m[k : k + 1, :] == expert
            named = named + jnp.where(hit, 1.0, 0.0)
            weight = weight + jnp.where(hit, m[8 + k : 9 + k, :], 0.0)
        before = ones_where(iota((toks, toks), 0) < iota((toks, toks), 1))
        rank = jnp.dot(named.astype(BF16), before, preferred_element_type=F32)
        taken = named > 0
        shift = (lax.rem(p, GROUP) * 2).astype(F32) - SUB
        in_main = jnp.where(taken & (rank < SUB), rank, -1.0)
        in_over = jnp.where(taken & (rank >= SUB), rank + shift, -1.0)
        row = iota((rows, 1), 0)
        spread = ones_where(lax.div(row, SUB) == iota((rows, lines), 1))
        within = lax.rem(row, SUB).astype(F32)
        placed = jnp.dot(spread, jnp.concatenate([in_main, in_over], axis=1).astype(BF16), preferred_element_type=F32)
        main, over = placed[:, :toks] == within, placed[:, toks:] == within
        high = weight.astype(BF16)
        rest = weight - high.astype(F32)
        mid = rest.astype(BF16)
        low = (rest - mid.astype(F32)).astype(BF16)
        spread_w = jnp.dot(
            jnp.concatenate([spread, spread, spread], axis=1),
            jnp.concatenate([high, mid, low], axis=0),
            preferred_element_type=F32,
        )
        pick_main[p] = ones_where(main)
        pick_over[p] = ones_where(over)
        gate_col[p] = jnp.sum(jnp.where(main, spread_w, 0.0), axis=1, keepdims=True)
        at = ZS + lax.div(p, GROUP)
        gate_col[at] = gate_col[at] + jnp.sum(jnp.where(over, spread_w, 0.0), axis=1, keepdims=True)
        return c

    def chunk_send(t, k, d):
        other = lax.rem(line + d, lines)
        return send(send_bufs[t].at[k % SLOTS_OUT, other], recv_bufs[t].at[k, line], pl_send.at[t, k], pl_recv.at[t, k], in_plane(other))

    def sent(t, k):
        rest = send_bufs[t].at[k % SLOTS_OUT, pl.ds(0, lines - 1)]
        return pltpu.make_async_copy(rest, rest, pl_send.at[t, k])

    def route(t, k, places):
        slot = k % SLOTS_OUT
        if k >= SLOTS_OUT:
            sent(t, k - SLOTS_OUT).wait()
        picks = pick_main if len(places) == 1 else pick_over
        total = None
        for p in places:
            part = jnp.dot(picks[p], gathered[t][p], preferred_element_type=F32)
            total = part if total is None else total + part
        if t == 1:
            total = total * gate_col[places[0] if len(places) == 1 else ZS + places[0] // GROUP]
        send_bufs[t][slot] = total.reshape(lines, SUB, width).astype(BF16)

        def go(d, c):
            chunk_send(t, k, d).start()
            return c

        lax.fori_loop(1, lines, go, 0)
        recv_bufs[t][k, line] = send_bufs[t][slot, line]

    def arrived(ref, sem):
        pltpu.make_async_copy(ref, ref, sem).wait()

    def expert(k):
        for t in (0, 1):
            arrived(recv_bufs[t].at[k, pl.ds(0, lines - 1)], pl_recv.at[t, k])
        x = in_x[k].reshape(rows, width)
        dy = in_g[k].reshape(rows, width)
        gate_pre = jnp.dot(x, weights[0], preferred_element_type=F32)
        up_pre = jnp.dot(x, weights[1], preferred_element_type=F32)
        hidden_grad = jnp.dot(dy, weights[2], preferred_element_type=F32)
        sig = jax.nn.sigmoid(gate_pre)
        active = gate_pre * sig
        hidden = (active * up_pre).astype(BF16)
        gate_grad = (hidden_grad * up_pre * sig * (1.0 + gate_pre * (1.0 - sig))).astype(BF16)
        up_grad = (hidden_grad * active).astype(BF16)
        acc[0] += lax.dot_general(x, gate_grad, contract_rows, preferred_element_type=F32)
        acc[1] += lax.dot_general(x, up_grad, contract_rows, preferred_element_type=F32)
        acc[2] += lax.dot_general(dy, hidden, contract_rows, preferred_element_type=F32)
        row_grad = lax.dot_general(
            gate_grad, weights[0], contract_cols, preferred_element_type=F32
        ) + lax.dot_general(up_grad, weights[1], contract_cols, preferred_element_type=F32)
        in_x[k] = row_grad.reshape(lines, SUB, width).astype(BF16)

    def give_back(k):
        def go(d, c):
            other = lax.rem(line + d, lines)
            send(in_x.at[k, other], back.at[k, line], rt_send.at[k], rt_recv.at[k], in_plane(other)).start()
            return c

        lax.fori_loop(1, lines, go, 0)
        back[k, line] = in_x[k, line]

    gate_col[...] = jnp.zeros_like(gate_col)
    prepare(0, 0)
    for t in (0, 1):
        own[t].wait()
        route(t, 0, (0,))
        if t == 0:
            both_ways(1, (0, 1), (0, 2))
    for m in metas:
        m.wait()
    lax.fori_loop(1, ZS, prepare, 0)
    acc[...] = jnp.zeros_like(acc)

    def work(k, c):
        @pl.when(k == 0)
        def _():
            for t in (0, 1):
                landed(t, (0, 1), (0, 2))
                both_ways(t, (1, 3), (2, 4))
                route(t, 1, (1,))
                route(t, 2, (2,))
            for i in range(3):
                w_local[i].wait()
                w_remote[i].wait()

        @pl.when(k == 1)
        def _():
            for t in (0, 1):
                landed(t, (1, 3), (2, 4))
                both_ways(t, (3, 5), (4, 6))
                route(t, 3, (3,))
                route(t, 4, (4,))
                route(t, 5, (0, 1, 2, 3))

        @pl.when(k == 3)
        def _():
            for t in (0, 1):
                landed(t, (3, 5), (4, 6))
                (hop(0, 5, 7, 1) if t == 0 else hop(1, 6, 7, -1)).start()
                route(t, 6, (5,))
                route(t, 7, (6,))
            for t in (0, 1):
                (hop(0, 5, 7, 1) if t == 0 else hop(1, 6, 7, -1)).wait_recv()
                route(t, 8, (7,))
                route(t, 9, (4, 5, 6, 7))

        expert(k)

        @pl.when(k == 8)
        def _():
            give_back(7)
            give_back(6)

        return c

    lax.fori_loop(0, CHUNKS, work, 0)
    give_back(9)
    give_back(8)

    def acc_rows(i, c):
        return acc.at[i, pl.ds(pl.multiple_of(c * depth, depth), depth)]

    acc_sends = [send(acc_rows(i, 1 - core), other_acc.at[i], a_send.at[i], a_recv.at[i], sibling) for i in range(3)]
    for s in acc_sends:
        s.start()

    def summed(p):
        return lax.dot_general(
            pick_main[p], back[MAIN[p]].reshape(rows, width), contract_rows, preferred_element_type=F32
        ) + lax.dot_general(
            pick_over[p], back[OVER[p // GROUP]].reshape(rows, width), contract_rows, preferred_element_type=F32
        )

    def returned(k):
        arrived(back.at[k, pl.ds(0, lines - 1)], rt_recv.at[k])

    def ring(p, dst, j):
        return send(stage.at[p], buf.at[dst], rs_send.at[dst], rs_recv.at[dst], along_z(j))

    low, high = pl.ds(0, half), pl.ds(half, half)
    returned(9)
    returned(8)
    part = summed(7)
    stage[7] = part.astype(BF16)
    r4 = send(stage.at[7, :, low], buf.at[6, :, low], rs_send.at[6], rs_recv.at[6], along_z(1))
    l4 = send(stage.at[7, :, high], buf.at[5, :, high], rs_send.at[5], rs_recv.at[5], along_z(-1))
    r4.start()
    l4.start()
    for k in (4, 5, 3, 2, 1, 0):
        give_back(k)
    returned(7)
    part = summed(6)
    r4.wait()
    stage[6, :, :half] = (part[:, :half] + buf[6, :, :half].astype(F32)).astype(BF16)
    stage[6, :, half:] = part[:, half:].astype(BF16)
    r3 = ring(6, 4, 1)
    r3.start()
    returned(6)
    part = summed(5)
    l4.wait()
    stage[5, :, :half] = part[:, :half].astype(BF16)
    stage[5, :, half:] = (part[:, half:] + buf[5, :, half:].astype(F32)).astype(BF16)
    l3 = ring(5, 3, -1)
    l3.start()

    outs = (gg_ref, gu_ref, gd_ref)
    stores = []
    for i in range(3):
        acc_sends[i].wait()
        other_acc[i] = other_acc[i] + acc[i, pl.ds(pl.multiple_of(core * depth, depth), depth), :]
        stores.append(pltpu.make_async_copy(other_acc.at[i], outs[i].at[0], own_sem.at[i]))
        stores[i].start()

    def forward(p, came):
        part = summed(p)
        came.wait()
        stage[p] = (part + buf[p].astype(F32)).astype(BF16)

    returned(4)
    forward(4, r3)
    r2 = ring(4, 2, 1)
    r2.start()
    returned(5)
    returned(3)
    forward(3, l3)
    l2 = ring(3, 1, -1)
    l2.start()
    returned(2)
    forward(2, r2)
    r1 = ring(2, 0, 1)
    r1.start()
    returned(1)
    forward(1, l2)
    l1 = ring(1, 7, -1)
    l1.start()
    returned(0)
    part = summed(0)
    r1.wait()
    l1.wait()
    out_ref[...] = (part + buf[0].astype(F32) + buf[7].astype(F32)).astype(BF16)

    for t in (0, 1):
        for src, dst in ((0, 1), (1, 3), (3, 5)) + (((5, 7),) if t == 0 else ()):
            hop(t, src, dst, 1).wait_send()
        for src, dst in ((0, 2), (2, 4), (4, 6)) + (((6, 7),) if t == 1 else ()):
            hop(t, src, dst, -1).wait_send()
        for k in range(CHUNKS - SLOTS_OUT, CHUNKS):
            sent(t, k).wait()
    for k in range(CHUNKS):
        rest = in_x.at[k, pl.ds(0, lines - 1)]
        arrived(rest, rt_send.at[k])
    for s in stores:
        s.wait()


def copies(*refs):
    n = len(refs) // 2
    sems = refs[-1]
    moves = [pltpu.make_async_copy(refs[i], refs[n + i], sems.at[i]) for i in range(n)]
    for m in moves:
        m.start()
    for m in moves:
        m.wait()


def local(tokens, out_grad, gates, expert_ids, w_gate, w_up, w_down):
    lines = lax.axis_size("expert") // ZS
    toks, width = tokens.shape
    depth, ff = w_gate.shape[1:]
    rows = lines * SUB
    any_spec = pl.BlockSpec(memory_space=pl.ANY)
    vmem = pl.BlockSpec(memory_space=pltpu.VMEM)
    dma = pltpu.SemaphoreType.DMA
    grads = jax.ShapeDtypeStruct((1, depth, ff), F32)
    results = pl.pallas_call(
        functools.partial(kernel, lines),
        out_shape=(jax.ShapeDtypeStruct((toks, width), BF16), grads, grads, grads),
        in_specs=[vmem] * 2 + [any_spec] * 5,
        out_specs=(vmem, any_spec, any_spec, any_spec),
        scratch_shapes=[
            pltpu.VMEM((ZS, 16, toks), F32),
            pltpu.VMEM((ZS, toks, width), BF16),
            pltpu.VMEM((ZS, toks, width), BF16),
            pltpu.VMEM((SLOTS_OUT, lines, SUB, width), BF16),
            pltpu.VMEM((SLOTS_OUT, lines, SUB, width), BF16),
            pltpu.VMEM((CHUNKS, lines, SUB, width), BF16),
            pltpu.VMEM((CHUNKS, lines, SUB, width), BF16),
            pltpu.VMEM((3, 2 * depth, ff), BF16),
            pltpu.VMEM((3, 2 * depth, ff), F32),
            pltpu.VMEM((3, depth, ff), F32),
            pltpu.VMEM((ZS, rows, toks), BF16),
            pltpu.VMEM((ZS, rows, toks), BF16),
            pltpu.VMEM((CHUNKS, rows, 1), F32),
            pltpu.VMEM((CHUNKS, lines, SUB, width), BF16),
            pltpu.VMEM((ZS, toks, width), BF16),
            pltpu.VMEM((ZS, toks, width), BF16),
            dma((ZS,)),
            dma((ZS,)),
            dma((2, ZS)),
            dma((2, ZS)),
            dma((2, CHUNKS)),
            dma((2, CHUNKS)),
            dma((CHUNKS,)),
            dma((CHUNKS,)),
            dma((3,)),
            dma((3,)),
            dma((3,)),
            dma((3,)),
            dma((ZS,)),
            dma((ZS,)),
            dma((5,)),
        ],
        compiler_params=pltpu.CompilerParams(
            collective_id=0, has_side_effects=True, vmem_limit_bytes=61 << 20
        ),
        name="experts_backward",
    )(expert_ids.T, gates.T, tokens, out_grad, w_gate, w_up, w_down)
    return pl.pallas_call(
        copies,
        out_shape=tuple(jax.ShapeDtypeStruct(r.shape, r.dtype) for r in results),
        in_specs=[any_spec] * 4,
        out_specs=(any_spec,) * 4,
        scratch_shapes=[dma((4,))],
        name="results",
    )(*results)


def solution(mesh):
    rows = P(("expert", "dp"), None)
    weights = P("expert", "dp", None)
    return jax.shard_map(
        local,
        mesh=mesh,
        in_specs=(rows, rows, rows, rows, weights, weights, weights),
        out_specs=(rows, weights, weights, weights),
        check_vma=False,
    )
```

```python
import functools

import jax
import jax.numpy as jnp
from jax import lax
from jax.experimental import pallas as pl
from jax.experimental.pallas import tpu as pltpu
from jax.sharding import PartitionSpec as P

BF16 = jnp.bfloat16
F32 = jnp.float32
MESH = pl.DeviceIdType.MESH
ZS = 8
SUB = 8
GROUP = 4

OFFSET = (0, -1, 1, -2, 2, -3, 3, 4)
MAIN = (0, 1, 2, 3, 4, 6, 7, 8)
OVER = (5, 9)
CHUNKS = 10
SLOTS_OUT = 6
PIECES = 4

contract_rows = (((0,), (0,)), ((), ()))
contract_cols = (((1,), (1,)), ((), ()))


def kernel(lines, ids_ref, gates_ref, tok_ref, grad_ref, wg_ref, wu_ref, wd_ref,
           out_ref, gg_ref, gu_ref, gd_ref,
           meta, block_x, block_g, out_x, out_g, in_x, in_g, weights, acc, other_acc,
           pick_main, pick_over, gate_col, back, stage, buf,
           meta_send, meta_recv, zs_send, zs_recv, pl_send, pl_recv, rt_send, rt_recv,
           w_send, w_recv, a_send, a_recv, rs_send, rs_recv, own_sem):
    me = lax.axis_index("expert")
    core = lax.axis_index("dp")
    z, line = lax.rem(me, ZS), lax.div(me, ZS)
    toks, width = tok_ref.shape
    depth = wg_ref.shape[1]
    rows = lines * SUB
    half = width // 2

    def along_z(j):
        return {"expert": line * ZS + lax.rem(z + j + 2 * ZS, ZS)}

    def in_plane(other):
        return {"expert": other * ZS + z}

    sibling = {"dp": 1 - core}

    def send(src, dst, send_sem, recv_sem, device):
        return pltpu.make_async_remote_copy(
            src_ref=src, dst_ref=dst, send_sem=send_sem, recv_sem=recv_sem,
            device_id=device, device_id_type=MESH,
        )

    barrier = pltpu.get_barrier_semaphore()

    def greet_line(j, c):
        pl.semaphore_signal(barrier, inc=1, device_id=along_z(j), device_id_type=MESH)
        return c

    def greet_plane(d, c):
        pl.semaphore_signal(barrier, inc=1, device_id=in_plane(lax.rem(line + d, lines)), device_id_type=MESH)
        return c

    lax.fori_loop(1, ZS, greet_line, 0)
    lax.fori_loop(1, lines, greet_plane, 0)
    pl.semaphore_signal(barrier, inc=1, device_id=sibling, device_id_type=MESH)

    sources = (tok_ref, grad_ref)
    gathered = (block_x, block_g)
    send_bufs = (out_x, out_g)
    recv_bufs = (in_x, in_g)

    def hop(t, src, dst, j):
        ref = sources[t] if src == 0 else gathered[t].at[src]
        return send(ref, gathered[t].at[dst], zs_send.at[t, dst], zs_recv.at[t, dst], along_z(j))

    def both_ways(t, right, left):
        for (src, dst), j in ((right, 1), (left, -1)):
            hop(t, src, dst, j).start()

    def landed(t, right, left):
        for (src, dst), j in ((right, 1), (left, -1)):
            hop(t, src, dst, j).wait_recv()

    own = [pltpu.make_async_copy(sources[t], gathered[t].at[0], own_sem.at[t]) for t in (0, 1)]
    metas = [send(meta.at[0], meta.at[p], meta_send.at[p], meta_recv.at[p], along_z(-OFFSET[p])) for p in range(1, ZS)]
    meta[0, :8] = ids_ref[...].astype(F32)
    meta[0, 8:] = gates_ref[...]
    for t in (0, 1):
        own[t].start()
    pl.semaphore_wait(barrier, ZS + lines - 1)
    both_ways(0, (0, 1), (0, 2))
    for m in metas:
        m.start()

    w_refs = (wg_ref, wu_ref, wd_ref)

    def mine(i):
        return weights.at[i, pl.ds(pl.multiple_of(core * depth, depth), depth)]

    w_remote = [send(w_refs[i].at[0], mine(i), w_send.at[i], w_recv.at[i], sibling) for i in range(3)]
    w_local = [pltpu.make_async_copy(w_refs[i].at[0], mine(i), own_sem.at[2 + i]) for i in range(3)]
    for i in range(3):
        w_local[i].start()

    def iota(shape, axis):
        return lax.broadcasted_iota(jnp.int32, shape, axis)

    def ones_where(mask):
        return jnp.where(mask, 1.0, 0.0).astype(BF16)

    def prepare(p, c):
        m = meta[p]
        expert = (iota((lines, toks), 0) * ZS + z).astype(F32)
        named = jnp.zeros((lines, toks), F32)
        weight = jnp.zeros((lines, toks), F32)
        for k in range(8):
            hit = m[k : k + 1, :] == expert
            named = named + jnp.where(hit, 1.0, 0.0)
            weight = weight + jnp.where(hit, m[8 + k : 9 + k, :], 0.0)
        before = ones_where(iota((toks, toks), 0) < iota((toks, toks), 1))
        rank = jnp.dot(named.astype(BF16), before, preferred_element_type=F32)
        taken = named > 0
        shift = (lax.rem(p, GROUP) * 2).astype(F32) - SUB
        in_main = jnp.where(taken & (rank < SUB), rank, -1.0)
        in_over = jnp.where(taken & (rank >= SUB), rank + shift, -1.0)
        row = iota((rows, 1), 0)
        spread = ones_where(lax.div(row, SUB) == iota((rows, lines), 1))
        within = lax.rem(row, SUB).astype(F32)
        placed = jnp.dot(spread, jnp.concatenate([in_main, in_over], axis=1).astype(BF16), preferred_element_type=F32)
        main, over = placed[:, :toks] == within, placed[:, toks:] == within
        high = weight.astype(BF16)
        rest = weight - high.astype(F32)
        mid = rest.astype(BF16)
        low = (rest - mid.astype(F32)).astype(BF16)
        spread_w = jnp.dot(
            jnp.concatenate([spread, spread, spread], axis=1),
            jnp.concatenate([high, mid, low], axis=0),
            preferred_element_type=F32,
        )
        pick_main[p] = ones_where(main)
        pick_over[p] = ones_where(over)
        gate_col[p] = jnp.sum(jnp.where(main, spread_w, 0.0), axis=1, keepdims=True)
        at = ZS + lax.div(p, GROUP)
        gate_col[at] = gate_col[at] + jnp.sum(jnp.where(over, spread_w, 0.0), axis=1, keepdims=True)
        return c

    def chunk_send(t, k, d):
        other = lax.rem(line + d, lines)
        return send(send_bufs[t].at[k % SLOTS_OUT, other], recv_bufs[t].at[k, line], pl_send.at[t, k], pl_recv.at[t, k], in_plane(other))

    def sent(t, k):
        rest = send_bufs[t].at[k % SLOTS_OUT, pl.ds(0, lines - 1)]
        return pltpu.make_async_copy(rest, rest, pl_send.at[t, k])

    def route(t, k, places):
        slot = k % SLOTS_OUT
        if k >= SLOTS_OUT:
            sent(t, k - SLOTS_OUT).wait()
        picks = pick_main if len(places) == 1 else pick_over
        total = None
        for p in places:
            part = jnp.dot(picks[p], gathered[t][p], preferred_element_type=F32)
            total = part if total is None else total + part
        if t == 1:
            total = total * gate_col[places[0] if len(places) == 1 else ZS + places[0] // GROUP]
        send_bufs[t][slot] = total.reshape(lines, SUB, width).astype(BF16)

        def go(d, c):
            chunk_send(t, k, d).start()
            return c

        lax.fori_loop(1, lines, go, 0)
        recv_bufs[t][k, line] = send_bufs[t][slot, line]

    def arrived(ref, sem):
        pltpu.make_async_copy(ref, ref, sem).wait()

    def expert(k):
        for t in (0, 1):
            arrived(recv_bufs[t].at[k, pl.ds(0, lines - 1)], pl_recv.at[t, k])
        x = in_x[k].reshape(rows, width)
        dy = in_g[k].reshape(rows, width)
        gate_pre = jnp.dot(x, weights[0], preferred_element_type=F32)
        up_pre = jnp.dot(x, weights[1], preferred_element_type=F32)
        hidden_grad = jnp.dot(dy, weights[2], preferred_element_type=F32)
        sig = jax.nn.sigmoid(gate_pre)
        active = gate_pre * sig
        hidden = (active * up_pre).astype(BF16)
        gate_grad = (hidden_grad * up_pre * sig * (1.0 + gate_pre * (1.0 - sig))).astype(BF16)
        up_grad = (hidden_grad * active).astype(BF16)
        acc[0] += lax.dot_general(x, gate_grad, contract_rows, preferred_element_type=F32)
        acc[1] += lax.dot_general(x, up_grad, contract_rows, preferred_element_type=F32)
        acc[2] += lax.dot_general(dy, hidden, contract_rows, preferred_element_type=F32)
        row_grad = lax.dot_general(
            gate_grad, weights[0], contract_cols, preferred_element_type=F32
        ) + lax.dot_general(up_grad, weights[1], contract_cols, preferred_element_type=F32)
        in_x[k] = row_grad.reshape(lines, SUB, width).astype(BF16)

    def give_back(k):
        def go(d, c):
            other = lax.rem(line + d, lines)
            send(in_x.at[k, other], back.at[k, line], rt_send.at[k], rt_recv.at[k], in_plane(other)).start()
            return c

        lax.fori_loop(1, lines, go, 0)
        back[k, line] = in_x[k, line]

    gate_col[...] = jnp.zeros_like(gate_col)
    prepare(0, 0)
    for t in (0, 1):
        own[t].wait()
        route(t, 0, (0,))
        if t == 0:
            both_ways(1, (0, 1), (0, 2))
    for m in metas:
        m.wait()
    lax.fori_loop(1, ZS, prepare, 0)
    acc[...] = jnp.zeros_like(acc)

    def work(k, c):
        @pl.when(k == 0)
        def _():
            for t in (0, 1):
                landed(t, (0, 1), (0, 2))
                both_ways(t, (1, 3), (2, 4))
                route(t, 1, (1,))
                route(t, 2, (2,))
            for i in range(3):
                w_remote[i].start()
            for t in (0, 1):
                landed(t, (1, 3), (2, 4))
                both_ways(t, (3, 5), (4, 6))
                route(t, 3, (3,))
                route(t, 4, (4,))
                route(t, 5, (0, 1, 2, 3))
            for i in range(3):
                w_local[i].wait()
                w_remote[i].wait()

        @pl.when(k == 3)
        def _():
            for t in (0, 1):
                landed(t, (3, 5), (4, 6))
                (hop(0, 5, 7, 1) if t == 0 else hop(1, 6, 7, -1)).start()
                route(t, 6, (5,))
                route(t, 7, (6,))
            for t in (0, 1):
                (hop(0, 5, 7, 1) if t == 0 else hop(1, 6, 7, -1)).wait_recv()
                route(t, 8, (7,))
                route(t, 9, (4, 5, 6, 7))

        expert(k)

        @pl.when(k == 8)
        def _():
            give_back(7)
            give_back(6)

        return c

    lax.fori_loop(0, CHUNKS, work, 0)
    give_back(9)
    give_back(8)

    def acc_rows(i, c):
        return acc.at[i, pl.ds(pl.multiple_of(c * depth, depth), depth)]

    acc_sends = [send(acc_rows(i, 1 - core), other_acc.at[i], a_send.at[i], a_recv.at[i], sibling) for i in range(3)]
    for s in acc_sends:
        s.start()

    def summed(p):
        return lax.dot_general(
            pick_main[p], back[MAIN[p]].reshape(rows, width), contract_rows, preferred_element_type=F32
        ) + lax.dot_general(
            pick_over[p], back[OVER[p // GROUP]].reshape(rows, width), contract_rows, preferred_element_type=F32
        )

    def returned(k):
        arrived(back.at[k, pl.ds(0, lines - 1)], rt_recv.at[k])

    def ring(p, dst, j):
        return send(stage.at[p], buf.at[dst], rs_send.at[dst], rs_recv.at[dst], along_z(j))

    low, high = pl.ds(0, half), pl.ds(half, half)
    returned(9)
    returned(8)
    part = summed(7)
    stage[7] = part.astype(BF16)
    r4 = send(stage.at[7, :, low], buf.at[6, :, low], rs_send.at[6], rs_recv.at[6], along_z(1))
    l4 = send(stage.at[7, :, high], buf.at[5, :, high], rs_send.at[5], rs_recv.at[5], along_z(-1))
    r4.start()
    l4.start()
    for k in (4, 5, 3, 2, 1, 0):
        give_back(k)
    returned(7)
    part = summed(6)
    r4.wait()
    stage[6, :, :half] = (part[:, :half] + buf[6, :, :half].astype(F32)).astype(BF16)
    stage[6, :, half:] = part[:, half:].astype(BF16)
    r3 = ring(6, 4, 1)
    r3.start()
    returned(6)
    part = summed(5)
    l4.wait()
    stage[5, :, :half] = part[:, :half].astype(BF16)
    stage[5, :, half:] = (part[:, half:] + buf[5, :, half:].astype(F32)).astype(BF16)
    l3 = ring(5, 3, -1)
    l3.start()

    outs = (gg_ref, gu_ref, gd_ref)
    stores = []
    for i in range(3):
        acc_sends[i].wait()
        other_acc[i] = other_acc[i] + acc[i, pl.ds(pl.multiple_of(core * depth, depth), depth), :]
        stores.append(pltpu.make_async_copy(other_acc.at[i], outs[i].at[0], own_sem.at[i]))
        stores[i].start()

    def forward(p, came):
        part = summed(p)
        came.wait()
        stage[p] = (part + buf[p].astype(F32)).astype(BF16)

    returned(4)
    forward(4, r3)
    r2 = ring(4, 2, 1)
    r2.start()
    returned(5)
    returned(3)
    forward(3, l3)
    l2 = ring(3, 1, -1)
    l2.start()
    returned(2)
    forward(2, r2)
    r1 = ring(2, 0, 1)
    r1.start()
    returned(1)
    forward(1, l2)
    l1 = ring(1, 7, -1)
    l1.start()
    returned(0)
    part = summed(0)
    r1.wait()
    l1.wait()
    out_ref[...] = (part + buf[0].astype(F32) + buf[7].astype(F32)).astype(BF16)

    for t in (0, 1):
        for src, dst in ((0, 1), (1, 3), (3, 5)) + (((5, 7),) if t == 0 else ()):
            hop(t, src, dst, 1).wait_send()
        for src, dst in ((0, 2), (2, 4), (4, 6)) + (((6, 7),) if t == 1 else ()):
            hop(t, src, dst, -1).wait_send()
        for k in range(CHUNKS - SLOTS_OUT, CHUNKS):
            sent(t, k).wait()
    for k in range(CHUNKS):
        rest = in_x.at[k, pl.ds(0, lines - 1)]
        arrived(rest, rt_send.at[k])
    for s in stores:
        s.wait()


def copies(*refs):
    n = 4
    came, left, held, sems = refs[:n], refs[n : 2 * n], refs[2 * n : 3 * n], refs[3 * n]
    parts = [(i, j) for j in range(PIECES) for i in range(n)]

    def move(src, dst, i, j, way):
        size = src[i].shape[-2] // PIECES
        at = (0,) * (len(src[i].shape) - 2) + (pl.ds(j * size, size),)
        return pltpu.make_async_copy(src[i].at[at], dst[i].at[at], sems.at[way, i, j])

    for i, j in parts:
        move(came, held, i, j, 0).start()
    for i, j in parts:
        move(came, held, i, j, 0).wait()
        move(held, left, i, j, 1).start()
    for i, j in parts:
        move(held, left, i, j, 1).wait()


def local(tokens, out_grad, gates, expert_ids, w_gate, w_up, w_down):
    lines = lax.axis_size("expert") // ZS
    toks, width = tokens.shape
    depth, ff = w_gate.shape[1:]
    rows = lines * SUB
    any_spec = pl.BlockSpec(memory_space=pl.ANY)
    vmem = pl.BlockSpec(memory_space=pltpu.VMEM)
    dma = pltpu.SemaphoreType.DMA
    grads = jax.ShapeDtypeStruct((1, depth, ff), F32)
    results = pl.pallas_call(
        functools.partial(kernel, lines),
        out_shape=(jax.ShapeDtypeStruct((toks, width), BF16), grads, grads, grads),
        in_specs=[vmem] * 2 + [any_spec] * 5,
        out_specs=(vmem, any_spec, any_spec, any_spec),
        scratch_shapes=[
            pltpu.VMEM((ZS, 16, toks), F32),
            pltpu.VMEM((ZS, toks, width), BF16),
            pltpu.VMEM((ZS, toks, width), BF16),
            pltpu.VMEM((SLOTS_OUT, lines, SUB, width), BF16),
            pltpu.VMEM((SLOTS_OUT, lines, SUB, width), BF16),
            pltpu.VMEM((CHUNKS, lines, SUB, width), BF16),
            pltpu.VMEM((CHUNKS, lines, SUB, width), BF16),
            pltpu.VMEM((3, 2 * depth, ff), BF16),
            pltpu.VMEM((3, 2 * depth, ff), F32),
            pltpu.VMEM((3, depth, ff), F32),
            pltpu.VMEM((ZS, rows, toks), BF16),
            pltpu.VMEM((ZS, rows, toks), BF16),
            pltpu.VMEM((CHUNKS, rows, 1), F32),
            pltpu.VMEM((CHUNKS, lines, SUB, width), BF16),
            pltpu.VMEM((ZS, toks, width), BF16),
            pltpu.VMEM((ZS, toks, width), BF16),
            dma((ZS,)),
            dma((ZS,)),
            dma((2, ZS)),
            dma((2, ZS)),
            dma((2, CHUNKS)),
            dma((2, CHUNKS)),
            dma((CHUNKS,)),
            dma((CHUNKS,)),
            dma((3,)),
            dma((3,)),
            dma((3,)),
            dma((3,)),
            dma((ZS,)),
            dma((ZS,)),
            dma((5,)),
        ],
        compiler_params=pltpu.CompilerParams(
            collective_id=0, has_side_effects=True, vmem_limit_bytes=61 << 20
        ),
        name="experts_backward",
    )(expert_ids.T, gates.T, tokens, out_grad, w_gate, w_up, w_down)
    return pl.pallas_call(
        copies,
        out_shape=tuple(jax.ShapeDtypeStruct(r.shape, r.dtype) for r in results),
        in_specs=[any_spec] * 4,
        out_specs=(any_spec,) * 4,
        scratch_shapes=[pltpu.VMEM(r.shape, r.dtype) for r in results] + [dma((2, 4, PIECES))],
        compiler_params=pltpu.CompilerParams(vmem_limit_bytes=60 << 20),
        name="results",
    )(*results)


def solution(mesh):
    rows = P(("expert", "dp"), None)
    weights = P("expert", "dp", None)
    return jax.shard_map(
        local,
        mesh=mesh,
        in_specs=(rows, rows, rows, rows, weights, weights, weights),
        out_specs=(rows, weights, weights, weights),
        check_vma=False,
    )
```

```python
import functools

import jax
import jax.numpy as jnp
from jax import lax
from jax.experimental import pallas as pl
from jax.experimental.pallas import tpu as pltpu
from jax.sharding import PartitionSpec as P

BF16 = jnp.bfloat16
F32 = jnp.float32
MESH = pl.DeviceIdType.MESH
ZS = 8
SUB = 8
GROUP = 4

OFFSET = (0, -1, 1, -2, 2, -3, 3, 4)
MAIN = (0, 1, 2, 3, 4, 5, 6, 7)
OVER = (9, 8)
CHUNKS = 10
SLOTS_OUT = 6
PIECES = 4

contract_rows = (((0,), (0,)), ((), ()))
contract_cols = (((1,), (1,)), ((), ()))


def kernel(lines, ids_ref, gates_ref, tok_ref, grad_ref, wg_ref, wu_ref, wd_ref,
           out_ref, gg_ref, gu_ref, gd_ref,
           meta, block_x, block_g, out_x, out_g, in_x, in_g, weights, acc, other_acc,
           pick_main, pick_over, gate_col, back, stage, buf,
           meta_send, meta_recv, zs_send, zs_recv, pl_send, pl_recv, rt_send, rt_recv,
           w_send, w_recv, a_send, a_recv, rs_send, rs_recv, own_sem):
    me = lax.axis_index("expert")
    core = lax.axis_index("dp")
    z, line = lax.rem(me, ZS), lax.div(me, ZS)
    toks, width = tok_ref.shape
    depth = wg_ref.shape[1]
    rows = lines * SUB
    half = width // 2

    def along_z(j):
        return {"expert": line * ZS + lax.rem(z + j + 2 * ZS, ZS)}

    def in_plane(other):
        return {"expert": other * ZS + z}

    sibling = {"dp": 1 - core}

    def send(src, dst, send_sem, recv_sem, device):
        return pltpu.make_async_remote_copy(
            src_ref=src, dst_ref=dst, send_sem=send_sem, recv_sem=recv_sem,
            device_id=device, device_id_type=MESH,
        )

    barrier = pltpu.get_barrier_semaphore()

    def greet_line(j, c):
        pl.semaphore_signal(barrier, inc=1, device_id=along_z(j), device_id_type=MESH)
        return c

    def greet_plane(d, c):
        pl.semaphore_signal(barrier, inc=1, device_id=in_plane(lax.rem(line + d, lines)), device_id_type=MESH)
        return c

    lax.fori_loop(1, ZS, greet_line, 0)
    lax.fori_loop(1, lines, greet_plane, 0)
    pl.semaphore_signal(barrier, inc=1, device_id=sibling, device_id_type=MESH)

    sources = (tok_ref, grad_ref)
    gathered = (block_x, block_g)
    send_bufs = (out_x, out_g)
    recv_bufs = (in_x, in_g)

    def hop(t, src, dst, j):
        ref = sources[t] if src == 0 else gathered[t].at[src]
        return send(ref, gathered[t].at[dst], zs_send.at[t, dst], zs_recv.at[t, dst], along_z(j))

    def both_ways(t, right, left):
        for (src, dst), j in ((right, 1), (left, -1)):
            hop(t, src, dst, j).start()

    def landed(t, right, left):
        for (src, dst), j in ((right, 1), (left, -1)):
            hop(t, src, dst, j).wait_recv()

    own = [pltpu.make_async_copy(sources[t], gathered[t].at[0], own_sem.at[t]) for t in (0, 1)]
    metas = [send(meta.at[0], meta.at[p], meta_send.at[p], meta_recv.at[p], along_z(-OFFSET[p])) for p in range(1, ZS)]
    meta[0, :8] = ids_ref[...].astype(F32)
    meta[0, 8:] = gates_ref[...]
    for t in (0, 1):
        own[t].start()
    w_refs = (wg_ref, wu_ref, wd_ref)

    def mine(i):
        return weights.at[i, pl.ds(pl.multiple_of(core * depth, depth), depth)]

    w_remote = [send(w_refs[i].at[0], mine(i), w_send.at[i], w_recv.at[i], sibling) for i in range(3)]
    w_local = [pltpu.make_async_copy(w_refs[i].at[0], mine(i), own_sem.at[2 + i]) for i in range(3)]
    for i in range(3):
        w_local[i].start()

    def iota(shape, axis):
        return lax.broadcasted_iota(jnp.int32, shape, axis)

    def ones_where(mask):
        return jnp.where(mask, 1.0, 0.0).astype(BF16)

    def prepare(p, c):
        m = meta[p]
        expert = (iota((lines, toks), 0) * ZS + z).astype(F32)
        named = jnp.zeros((lines, toks), F32)
        weight = jnp.zeros((lines, toks), F32)
        for k in range(8):
            hit = m[k : k + 1, :] == expert
            named = named + jnp.where(hit, 1.0, 0.0)
            weight = weight + jnp.where(hit, m[8 + k : 9 + k, :], 0.0)
        before = ones_where(iota((toks, toks), 0) < iota((toks, toks), 1))
        rank = jnp.dot(named.astype(BF16), before, preferred_element_type=F32)
        taken = named > 0
        shift = (lax.rem(p, GROUP) * 2).astype(F32) - SUB
        in_main = jnp.where(taken & (rank < SUB), rank, -1.0)
        in_over = jnp.where(taken & (rank >= SUB), rank + shift, -1.0)
        row = iota((rows, 1), 0)
        spread = ones_where(lax.div(row, SUB) == iota((rows, lines), 1))
        within = lax.rem(row, SUB).astype(F32)
        placed = jnp.dot(spread, jnp.concatenate([in_main, in_over], axis=1).astype(BF16), preferred_element_type=F32)
        main, over = placed[:, :toks] == within, placed[:, toks:] == within
        high = weight.astype(BF16)
        rest = weight - high.astype(F32)
        mid = rest.astype(BF16)
        low = (rest - mid.astype(F32)).astype(BF16)
        spread_w = jnp.dot(
            jnp.concatenate([spread, spread, spread], axis=1),
            jnp.concatenate([high, mid, low], axis=0),
            preferred_element_type=F32,
        )
        pick_main[p] = ones_where(main)
        pick_over[p] = ones_where(over)
        gate_col[p] = jnp.sum(jnp.where(main, spread_w, 0.0), axis=1, keepdims=True)
        at = ZS + lax.div(p, GROUP)
        gate_col[at] = gate_col[at] + jnp.sum(jnp.where(over, spread_w, 0.0), axis=1, keepdims=True)
        return c

    gate_col[...] = jnp.zeros_like(gate_col)
    prepare(0, 0)

    pl.semaphore_wait(barrier, ZS + lines - 1)
    both_ways(0, (0, 1), (0, 2))
    for m in metas:
        m.start()

    def chunk_send(t, k, d):
        other = lax.rem(line + d, lines)
        return send(send_bufs[t].at[k % SLOTS_OUT, other], recv_bufs[t].at[k, line], pl_send.at[t, k], pl_recv.at[t, k], in_plane(other))

    def sent(t, k):
        rest = send_bufs[t].at[k % SLOTS_OUT, pl.ds(0, lines - 1)]
        return pltpu.make_async_copy(rest, rest, pl_send.at[t, k])

    def route(t, k, places):
        slot = k % SLOTS_OUT
        if k >= SLOTS_OUT:
            sent(t, k - SLOTS_OUT).wait()
        picks = pick_main if len(places) == 1 else pick_over
        total = None
        for p in places:
            part = jnp.dot(picks[p], gathered[t][p], preferred_element_type=F32)
            total = part if total is None else total + part
        if t == 1:
            total = total * gate_col[places[0] if len(places) == 1 else ZS + places[0] // GROUP]
        send_bufs[t][slot] = total.reshape(lines, SUB, width).astype(BF16)

        def go(d, c):
            chunk_send(t, k, d).start()
            return c

        lax.fori_loop(1, lines, go, 0)
        recv_bufs[t][k, line] = send_bufs[t][slot, line]

    def arrived(ref, sem):
        pltpu.make_async_copy(ref, ref, sem).wait()

    def expert(k):
        for t in (0, 1):
            arrived(recv_bufs[t].at[k, pl.ds(0, lines - 1)], pl_recv.at[t, k])
        x = in_x[k].reshape(rows, width)
        dy = in_g[k].reshape(rows, width)
        gate_pre = jnp.dot(x, weights[0], preferred_element_type=F32)
        up_pre = jnp.dot(x, weights[1], preferred_element_type=F32)
        hidden_grad = jnp.dot(dy, weights[2], preferred_element_type=F32)
        sig = jax.nn.sigmoid(gate_pre)
        active = gate_pre * sig
        hidden = (active * up_pre).astype(BF16)
        gate_grad = (hidden_grad * up_pre * sig * (1.0 + gate_pre * (1.0 - sig))).astype(BF16)
        up_grad = (hidden_grad * active).astype(BF16)
        acc[0] += lax.dot_general(x, gate_grad, contract_rows, preferred_element_type=F32)
        acc[1] += lax.dot_general(x, up_grad, contract_rows, preferred_element_type=F32)
        acc[2] += lax.dot_general(dy, hidden, contract_rows, preferred_element_type=F32)
        row_grad = lax.dot_general(
            gate_grad, weights[0], contract_cols, preferred_element_type=F32
        ) + lax.dot_general(up_grad, weights[1], contract_cols, preferred_element_type=F32)
        in_x[k] = row_grad.reshape(lines, SUB, width).astype(BF16)

    def give_back(k):
        def go(d, c):
            other = lax.rem(line + d, lines)
            send(in_x.at[k, other], back.at[k, line], rt_send.at[k], rt_recv.at[k], in_plane(other)).start()
            return c

        lax.fori_loop(1, lines, go, 0)
        back[k, line] = in_x[k, line]

    for t in (0, 1):
        own[t].wait()
        route(t, 0, (0,))
        if t == 0:
            both_ways(1, (0, 1), (0, 2))
    for m in metas:
        m.wait()
    lax.fori_loop(1, ZS, prepare, 0)
    acc[...] = jnp.zeros_like(acc)

    def work(k, c):
        @pl.when(k == 0)
        def _():
            for t in (0, 1):
                landed(t, (0, 1), (0, 2))
                both_ways(t, (1, 3), (2, 4))
                route(t, 1, (1,))
                route(t, 2, (2,))
            for i in range(3):
                w_remote[i].start()
            for t in (0, 1):
                landed(t, (1, 3), (2, 4))
                both_ways(t, (3, 5), (4, 6))
                route(t, 3, (3,))
                route(t, 4, (4,))
            for i in range(3):
                w_local[i].wait()
                w_remote[i].wait()

        @pl.when(k == 3)
        def _():
            for t in (0, 1):
                landed(t, (3, 5), (4, 6))
                (hop(0, 5, 7, 1) if t == 0 else hop(1, 6, 7, -1)).start()
                route(t, 5, (5,))
                route(t, 6, (6,))
            for t in (0, 1):
                (hop(0, 5, 7, 1) if t == 0 else hop(1, 6, 7, -1)).wait_recv()
                route(t, 7, (7,))
                route(t, 8, (4, 5, 6, 7))
            for t in (0, 1):
                route(t, 9, (0, 1, 2, 3))

        expert(k)

        @pl.when(k == 8)
        def _():
            give_back(7)
            give_back(8)

        return c

    lax.fori_loop(0, CHUNKS, work, 0)
    give_back(6)
    give_back(5)

    def acc_rows(i, c):
        return acc.at[i, pl.ds(pl.multiple_of(c * depth, depth), depth)]

    acc_sends = [send(acc_rows(i, 1 - core), other_acc.at[i], a_send.at[i], a_recv.at[i], sibling) for i in range(3)]
    for s in acc_sends:
        s.start()

    def summed(p):
        return lax.dot_general(
            pick_main[p], back[MAIN[p]].reshape(rows, width), contract_rows, preferred_element_type=F32
        ) + lax.dot_general(
            pick_over[p], back[OVER[p // GROUP]].reshape(rows, width), contract_rows, preferred_element_type=F32
        )

    def returned(k):
        arrived(back.at[k, pl.ds(0, lines - 1)], rt_recv.at[k])

    def ring(p, dst, j):
        return send(stage.at[p], buf.at[dst], rs_send.at[dst], rs_recv.at[dst], along_z(j))

    low, high = pl.ds(0, half), pl.ds(half, half)
    returned(8)
    returned(7)
    part = summed(7)
    stage[7] = part.astype(BF16)
    r4 = send(stage.at[7, :, low], buf.at[6, :, low], rs_send.at[6], rs_recv.at[6], along_z(1))
    l4 = send(stage.at[7, :, high], buf.at[5, :, high], rs_send.at[5], rs_recv.at[5], along_z(-1))
    r4.start()
    l4.start()
    for k in (4, 9, 3, 2, 1, 0):
        give_back(k)
    returned(6)
    part = summed(6)
    r4.wait()
    stage[6, :, :half] = (part[:, :half] + buf[6, :, :half].astype(F32)).astype(BF16)
    stage[6, :, half:] = part[:, half:].astype(BF16)
    r3 = ring(6, 4, 1)
    r3.start()
    returned(5)
    part = summed(5)
    l4.wait()
    stage[5, :, :half] = part[:, :half].astype(BF16)
    stage[5, :, half:] = (part[:, half:] + buf[5, :, half:].astype(F32)).astype(BF16)
    l3 = ring(5, 3, -1)
    l3.start()

    outs = (gg_ref, gu_ref, gd_ref)
    stores = []
    for i in range(3):
        acc_sends[i].wait()
        other_acc[i] = other_acc[i] + acc[i, pl.ds(pl.multiple_of(core * depth, depth), depth), :]
        stores.append(pltpu.make_async_copy(other_acc.at[i], outs[i].at[0], own_sem.at[i]))
        stores[i].start()

    def forward(p, came):
        part = summed(p)
        came.wait()
        stage[p] = (part + buf[p].astype(F32)).astype(BF16)

    returned(4)
    forward(4, r3)
    r2 = ring(4, 2, 1)
    r2.start()
    returned(9)
    returned(3)
    forward(3, l3)
    l2 = ring(3, 1, -1)
    l2.start()
    returned(2)
    forward(2, r2)
    r1 = ring(2, 0, 1)
    r1.start()
    returned(1)
    forward(1, l2)
    l1 = ring(1, 7, -1)
    l1.start()
    returned(0)
    part = summed(0)
    r1.wait()
    l1.wait()
    out_ref[...] = (part + buf[0].astype(F32) + buf[7].astype(F32)).astype(BF16)

    for t in (0, 1):
        for src, dst in ((0, 1), (1, 3), (3, 5)) + (((5, 7),) if t == 0 else ()):
            hop(t, src, dst, 1).wait_send()
        for src, dst in ((0, 2), (2, 4), (4, 6)) + (((6, 7),) if t == 1 else ()):
            hop(t, src, dst, -1).wait_send()
        for k in range(CHUNKS - SLOTS_OUT, CHUNKS):
            sent(t, k).wait()
    for k in range(CHUNKS):
        rest = in_x.at[k, pl.ds(0, lines - 1)]
        arrived(rest, rt_send.at[k])
    for s in stores:
        s.wait()


def copies(*refs):
    n = 4
    came, left, held, sems = refs[:n], refs[n : 2 * n], refs[2 * n : 3 * n], refs[3 * n]
    parts = [(i, j) for j in range(PIECES) for i in range(n)]

    def move(src, dst, i, j, way):
        size = src[i].shape[-2] // PIECES
        at = (0,) * (len(src[i].shape) - 2) + (pl.ds(j * size, size),)
        return pltpu.make_async_copy(src[i].at[at], dst[i].at[at], sems.at[way, i, j])

    for i, j in parts:
        move(came, held, i, j, 0).start()
    for i, j in parts:
        move(came, held, i, j, 0).wait()
        move(held, left, i, j, 1).start()
    for i, j in parts:
        move(held, left, i, j, 1).wait()


def local(tokens, out_grad, gates, expert_ids, w_gate, w_up, w_down):
    lines = lax.axis_size("expert") // ZS
    toks, width = tokens.shape
    depth, ff = w_gate.shape[1:]
    rows = lines * SUB
    any_spec = pl.BlockSpec(memory_space=pl.ANY)
    vmem = pl.BlockSpec(memory_space=pltpu.VMEM)
    dma = pltpu.SemaphoreType.DMA
    grads = jax.ShapeDtypeStruct((1, depth, ff), F32)
    results = pl.pallas_call(
        functools.partial(kernel, lines),
        out_shape=(jax.ShapeDtypeStruct((toks, width), BF16), grads, grads, grads),
        in_specs=[vmem] * 2 + [any_spec] * 5,
        out_specs=(vmem, any_spec, any_spec, any_spec),
        scratch_shapes=[
            pltpu.VMEM((ZS, 16, toks), F32),
            pltpu.VMEM((ZS, toks, width), BF16),
            pltpu.VMEM((ZS, toks, width), BF16),
            pltpu.VMEM((SLOTS_OUT, lines, SUB, width), BF16),
            pltpu.VMEM((SLOTS_OUT, lines, SUB, width), BF16),
            pltpu.VMEM((CHUNKS, lines, SUB, width), BF16),
            pltpu.VMEM((CHUNKS, lines, SUB, width), BF16),
            pltpu.VMEM((3, 2 * depth, ff), BF16),
            pltpu.VMEM((3, 2 * depth, ff), F32),
            pltpu.VMEM((3, depth, ff), F32),
            pltpu.VMEM((ZS, rows, toks), BF16),
            pltpu.VMEM((ZS, rows, toks), BF16),
            pltpu.VMEM((CHUNKS, rows, 1), F32),
            pltpu.VMEM((CHUNKS, lines, SUB, width), BF16),
            pltpu.VMEM((ZS, toks, width), BF16),
            pltpu.VMEM((ZS, toks, width), BF16),
            dma((ZS,)),
            dma((ZS,)),
            dma((2, ZS)),
            dma((2, ZS)),
            dma((2, CHUNKS)),
            dma((2, CHUNKS)),
            dma((CHUNKS,)),
            dma((CHUNKS,)),
            dma((3,)),
            dma((3,)),
            dma((3,)),
            dma((3,)),
            dma((ZS,)),
            dma((ZS,)),
            dma((5,)),
        ],
        compiler_params=pltpu.CompilerParams(
            collective_id=0, has_side_effects=True, vmem_limit_bytes=61 << 20
        ),
        name="experts_backward",
    )(expert_ids.T, gates.T, tokens, out_grad, w_gate, w_up, w_down)
    return pl.pallas_call(
        copies,
        out_shape=tuple(jax.ShapeDtypeStruct(r.shape, r.dtype) for r in results),
        in_specs=[any_spec] * 4,
        out_specs=(any_spec,) * 4,
        scratch_shapes=[pltpu.VMEM(r.shape, r.dtype) for r in results] + [dma((2, 4, PIECES))],
        compiler_params=pltpu.CompilerParams(vmem_limit_bytes=60 << 20),
        name="results",
    )(*results)


def solution(mesh):
    rows = P(("expert", "dp"), None)
    weights = P("expert", "dp", None)
    return jax.shard_map(
        local,
        mesh=mesh,
        in_specs=(rows, rows, rows, rows, weights, weights, weights),
        out_specs=(rows, weights, weights, weights),
        check_vma=False,
    )
```

```python
import functools

import jax
import jax.numpy as jnp
from jax import lax
from jax.experimental import pallas as pl
from jax.experimental.pallas import tpu as pltpu
from jax.sharding import PartitionSpec as P

BF16 = jnp.bfloat16
F32 = jnp.float32
MESH = pl.DeviceIdType.MESH
ZS = 8
SUB = 8
GROUP = 4

OFFSET = (0, -1, 1, -2, 2, -3, 3, 4)
MAIN = (0, 1, 2, 3, 4, 5, 6, 7)
OVER = (9, 8)
CHUNKS = 10
SLOTS_OUT = 6
PIECES = 4

contract_rows = (((0,), (0,)), ((), ()))
contract_cols = (((1,), (1,)), ((), ()))


def kernel(lines, ids_ref, gates_ref, tok_ref, grad_ref, wg_ref, wu_ref, wd_ref,
           out_ref, gg_ref, gu_ref, gd_ref,
           meta, block_x, block_g, out_x, out_g, in_x, in_g, weights, acc, other_acc,
           pick_main, pick_over, gate_col, back, stage, buf,
           meta_send, meta_recv, zs_send, zs_recv, pl_send, pl_recv, rt_send, rt_recv,
           w_send, w_recv, a_send, a_recv, rs_send, rs_recv, own_sem):
    me = lax.axis_index("expert")
    core = lax.axis_index("dp")
    z, line = lax.rem(me, ZS), lax.div(me, ZS)
    toks, width = tok_ref.shape
    depth = wg_ref.shape[1]
    rows = lines * SUB
    half = width // 2

    def along_z(j):
        return {"expert": line * ZS + lax.rem(z + j + 2 * ZS, ZS)}

    def in_plane(other):
        return {"expert": other * ZS + z}

    sibling = {"dp": 1 - core}

    def send(src, dst, send_sem, recv_sem, device):
        return pltpu.make_async_remote_copy(
            src_ref=src, dst_ref=dst, send_sem=send_sem, recv_sem=recv_sem,
            device_id=device, device_id_type=MESH,
        )

    barrier = pltpu.get_barrier_semaphore()

    def greet_line(j, c):
        pl.semaphore_signal(barrier, inc=1, device_id=along_z(j), device_id_type=MESH)
        return c

    def greet_plane(d, c):
        pl.semaphore_signal(barrier, inc=1, device_id=in_plane(lax.rem(line + d, lines)), device_id_type=MESH)
        return c

    lax.fori_loop(1, ZS, greet_line, 0)
    lax.fori_loop(1, lines, greet_plane, 0)
    pl.semaphore_signal(barrier, inc=1, device_id=sibling, device_id_type=MESH)

    sources = (tok_ref, grad_ref)
    gathered = (block_x, block_g)
    send_bufs = (out_x, out_g)
    recv_bufs = (in_x, in_g)

    def hop(t, src, dst, j):
        ref = sources[t] if src == 0 else gathered[t].at[src]
        return send(ref, gathered[t].at[dst], zs_send.at[t, dst], zs_recv.at[t, dst], along_z(j))

    def both_ways(t, right, left):
        for (src, dst), j in ((right, 1), (left, -1)):
            hop(t, src, dst, j).start()

    def landed(t, right, left):
        for (src, dst), j in ((right, 1), (left, -1)):
            hop(t, src, dst, j).wait_recv()

    own = [pltpu.make_async_copy(sources[t], gathered[t].at[0], own_sem.at[t]) for t in (0, 1)]
    metas = [send(meta.at[0], meta.at[p], meta_send.at[p], meta_recv.at[p], along_z(-OFFSET[p])) for p in range(1, ZS)]
    meta[0, :8] = ids_ref[...].astype(F32)
    meta[0, 8:] = gates_ref[...]
    for t in (0, 1):
        own[t].start()
    w_refs = (wg_ref, wu_ref, wd_ref)

    def mine(i):
        return weights.at[i, pl.ds(pl.multiple_of(core * depth, depth), depth)]

    w_remote = [send(w_refs[i].at[0], mine(i), w_send.at[i], w_recv.at[i], sibling) for i in range(3)]
    w_local = [pltpu.make_async_copy(w_refs[i].at[0], mine(i), own_sem.at[2 + i]) for i in range(3)]
    for i in range(3):
        w_local[i].start()

    def iota(shape, axis):
        return lax.broadcasted_iota(jnp.int32, shape, axis)

    def ones_where(mask):
        return jnp.where(mask, 1.0, 0.0).astype(BF16)

    def prepare(p, c):
        m = meta[p]
        expert = (iota((lines, toks), 0) * ZS + z).astype(F32)
        named = jnp.zeros((lines, toks), F32)
        weight = jnp.zeros((lines, toks), F32)
        for k in range(8):
            hit = m[k : k + 1, :] == expert
            named = named + jnp.where(hit, 1.0, 0.0)
            weight = weight + jnp.where(hit, m[8 + k : 9 + k, :], 0.0)
        before = ones_where(iota((toks, toks), 0) < iota((toks, toks), 1))
        rank = jnp.dot(named.astype(BF16), before, preferred_element_type=F32)
        taken = named > 0
        shift = (lax.rem(p, GROUP) * 2).astype(F32) - SUB
        in_main = jnp.where(taken & (rank < SUB), rank, -1.0)
        in_over = jnp.where(taken & (rank >= SUB), rank + shift, -1.0)
        row = iota((rows, 1), 0)
        spread = ones_where(lax.div(row, SUB) == iota((rows, lines), 1))
        within = lax.rem(row, SUB).astype(F32)
        placed = jnp.dot(spread, jnp.concatenate([in_main, in_over], axis=1).astype(BF16), preferred_element_type=F32)
        main, over = placed[:, :toks] == within, placed[:, toks:] == within
        high = weight.astype(BF16)
        rest = weight - high.astype(F32)
        mid = rest.astype(BF16)
        low = (rest - mid.astype(F32)).astype(BF16)
        spread_w = jnp.dot(
            jnp.concatenate([spread, spread, spread], axis=1),
            jnp.concatenate([high, mid, low], axis=0),
            preferred_element_type=F32,
        )
        pick_main[p] = ones_where(main)
        pick_over[p] = ones_where(over)
        gate_col[p] = jnp.sum(jnp.where(main, spread_w, 0.0), axis=1, keepdims=True)
        at = ZS + lax.div(p, GROUP)
        gate_col[at] = gate_col[at] + jnp.sum(jnp.where(over, spread_w, 0.0), axis=1, keepdims=True)
        return c

    gate_col[...] = jnp.zeros_like(gate_col)
    prepare(0, 0)

    pl.semaphore_wait(barrier, ZS + lines - 1)
    both_ways(0, (0, 1), (0, 2))
    for m in metas:
        m.start()

    def chunk_send(t, k, d):
        other = lax.rem(line + d, lines)
        return send(send_bufs[t].at[k % SLOTS_OUT, other], recv_bufs[t].at[k, line], pl_send.at[t, k], pl_recv.at[t, k], in_plane(other))

    def sent(t, k):
        rest = send_bufs[t].at[k % SLOTS_OUT, pl.ds(0, lines - 1)]
        return pltpu.make_async_copy(rest, rest, pl_send.at[t, k])

    def route(t, k, places):
        slot = k % SLOTS_OUT
        if k >= SLOTS_OUT:
            sent(t, k - SLOTS_OUT).wait()
        picks = pick_main if len(places) == 1 else pick_over
        total = None
        for p in places:
            part = jnp.dot(picks[p], gathered[t][p], preferred_element_type=F32)
            total = part if total is None else total + part
        if t == 1:
            total = total * gate_col[places[0] if len(places) == 1 else ZS + places[0] // GROUP]
        send_bufs[t][slot] = total.reshape(lines, SUB, width).astype(BF16)

        def go(d, c):
            chunk_send(t, k, d).start()
            return c

        lax.fori_loop(1, lines, go, 0)
        recv_bufs[t][k, line] = send_bufs[t][slot, line]

    def arrived(ref, sem):
        pltpu.make_async_copy(ref, ref, sem).wait()

    def expert(k):
        for t in (0, 1):
            arrived(recv_bufs[t].at[k, pl.ds(0, lines - 1)], pl_recv.at[t, k])
        x = in_x[k].reshape(rows, width)
        dy = in_g[k].reshape(rows, width)
        gate_pre = jnp.dot(x, weights[0], preferred_element_type=F32)
        up_pre = jnp.dot(x, weights[1], preferred_element_type=F32)
        hidden_grad = jnp.dot(dy, weights[2], preferred_element_type=F32)
        sig = jax.nn.sigmoid(gate_pre)
        active = gate_pre * sig
        hidden = (active * up_pre).astype(BF16)
        gate_grad = (hidden_grad * up_pre * sig * (1.0 + gate_pre * (1.0 - sig))).astype(BF16)
        up_grad = (hidden_grad * active).astype(BF16)
        acc[0] += lax.dot_general(x, gate_grad, contract_rows, preferred_element_type=F32)
        acc[1] += lax.dot_general(x, up_grad, contract_rows, preferred_element_type=F32)
        acc[2] += lax.dot_general(dy, hidden, contract_rows, preferred_element_type=F32)
        row_grad = lax.dot_general(
            gate_grad, weights[0], contract_cols, preferred_element_type=F32
        ) + lax.dot_general(up_grad, weights[1], contract_cols, preferred_element_type=F32)
        in_x[k] = row_grad.reshape(lines, SUB, width).astype(BF16)

    def give_back(k):
        def go(d, c):
            other = lax.rem(line + d, lines)
            send(in_x.at[k, other], back.at[k, line], rt_send.at[k], rt_recv.at[k], in_plane(other)).start()
            return c

        lax.fori_loop(1, lines, go, 0)
        back[k, line] = in_x[k, line]

    for t in (0, 1):
        own[t].wait()
        route(t, 0, (0,))
        if t == 0:
            both_ways(1, (0, 1), (0, 2))
    for m in metas:
        m.wait()
    lax.fori_loop(1, 3, prepare, 0)

    def work(k, c):
        @pl.when(k == 0)
        def _():
            for t in (0, 1):
                landed(t, (0, 1), (0, 2))
                both_ways(t, (1, 3), (2, 4))
                route(t, 1, (1,))
                route(t, 2, (2,))
                if t == 0:
                    lax.fori_loop(3, ZS, prepare, 0)
            for i in range(3):
                w_remote[i].start()
            acc[...] = jnp.zeros_like(acc)
            for t in (0, 1):
                landed(t, (1, 3), (2, 4))
                both_ways(t, (3, 5), (4, 6))
                route(t, 3, (3,))
                route(t, 4, (4,))
            for i in range(3):
                w_local[i].wait()
                w_remote[i].wait()

        @pl.when(k == 3)
        def _():
            for t in (0, 1):
                landed(t, (3, 5), (4, 6))
                (hop(0, 5, 7, 1) if t == 0 else hop(1, 6, 7, -1)).start()
                route(t, 5, (5,))
                route(t, 6, (6,))

        @pl.when(k == 4)
        def _():
            for t in (0, 1):
                (hop(0, 5, 7, 1) if t == 0 else hop(1, 6, 7, -1)).wait_recv()
                route(t, 7, (7,))
                route(t, 8, (4, 5, 6, 7))
            for t in (0, 1):
                route(t, 9, (0, 1, 2, 3))

        expert(k)

        @pl.when(k == 8)
        def _():
            give_back(7)
            give_back(8)

        return c

    lax.fori_loop(0, CHUNKS, work, 0)
    give_back(6)
    give_back(5)

    def acc_rows(i, c):
        return acc.at[i, pl.ds(pl.multiple_of(c * depth, depth), depth)]

    acc_sends = [send(acc_rows(i, 1 - core), other_acc.at[i], a_send.at[i], a_recv.at[i], sibling) for i in range(3)]

    def summed(p):
        return lax.dot_general(
            pick_main[p], back[MAIN[p]].reshape(rows, width), contract_rows, preferred_element_type=F32
        ) + lax.dot_general(
            pick_over[p], back[OVER[p // GROUP]].reshape(rows, width), contract_rows, preferred_element_type=F32
        )

    def returned(k):
        arrived(back.at[k, pl.ds(0, lines - 1)], rt_recv.at[k])

    def ring(p, dst, j):
        return send(stage.at[p], buf.at[dst], rs_send.at[dst], rs_recv.at[dst], along_z(j))

    low, high = pl.ds(0, half), pl.ds(half, half)
    returned(8)
    returned(7)
    part = summed(7)
    stage[7] = part.astype(BF16)
    r4 = send(stage.at[7, :, low], buf.at[6, :, low], rs_send.at[6], rs_recv.at[6], along_z(1))
    l4 = send(stage.at[7, :, high], buf.at[5, :, high], rs_send.at[5], rs_recv.at[5], along_z(-1))
    r4.start()
    l4.start()
    for k in (4, 9, 3, 2, 1, 0):
        give_back(k)
    for s in acc_sends:
        s.start()
    returned(6)
    part = summed(6)
    r4.wait()
    stage[6, :, :half] = (part[:, :half] + buf[6, :, :half].astype(F32)).astype(BF16)
    stage[6, :, half:] = part[:, half:].astype(BF16)
    r3 = ring(6, 4, 1)
    r3.start()
    returned(5)
    part = summed(5)
    l4.wait()
    stage[5, :, :half] = part[:, :half].astype(BF16)
    stage[5, :, half:] = (part[:, half:] + buf[5, :, half:].astype(F32)).astype(BF16)
    l3 = ring(5, 3, -1)
    l3.start()

    def forward(p, came):
        part = summed(p)
        came.wait()
        stage[p] = (part + buf[p].astype(F32)).astype(BF16)

    returned(4)
    forward(4, r3)
    r2 = ring(4, 2, 1)
    r2.start()
    returned(9)
    returned(3)
    forward(3, l3)
    l2 = ring(3, 1, -1)
    l2.start()
    returned(2)
    forward(2, r2)
    r1 = ring(2, 0, 1)
    r1.start()
    returned(1)
    forward(1, l2)
    l1 = ring(1, 7, -1)
    l1.start()
    outs = (gg_ref, gu_ref, gd_ref)
    stores = []
    for i in range(3):
        acc_sends[i].wait()
        other_acc[i] = other_acc[i] + acc[i, pl.ds(pl.multiple_of(core * depth, depth), depth), :]
        stores.append(pltpu.make_async_copy(other_acc.at[i], outs[i].at[0], own_sem.at[i]))
        stores[i].start()
    returned(0)
    part = summed(0)
    r1.wait()
    l1.wait()
    out_ref[...] = (part + buf[0].astype(F32) + buf[7].astype(F32)).astype(BF16)

    for t in (0, 1):
        for src, dst in ((0, 1), (1, 3), (3, 5)) + (((5, 7),) if t == 0 else ()):
            hop(t, src, dst, 1).wait_send()
        for src, dst in ((0, 2), (2, 4), (4, 6)) + (((6, 7),) if t == 1 else ()):
            hop(t, src, dst, -1).wait_send()
        for k in range(CHUNKS - SLOTS_OUT, CHUNKS):
            sent(t, k).wait()
    for k in range(CHUNKS):
        rest = in_x.at[k, pl.ds(0, lines - 1)]
        arrived(rest, rt_send.at[k])
    for s in stores:
        s.wait()


def copies(*refs):
    n = 4
    came, left, held, sems = refs[:n], refs[n : 2 * n], refs[2 * n : 3 * n], refs[3 * n]
    parts = [(i, j) for j in range(PIECES) for i in range(n)]

    def move(src, dst, i, j, way):
        size = src[i].shape[-2] // PIECES
        at = (0,) * (len(src[i].shape) - 2) + (pl.ds(j * size, size),)
        return pltpu.make_async_copy(src[i].at[at], dst[i].at[at], sems.at[way, i, j])

    for i, j in parts:
        move(came, held, i, j, 0).start()
    for i, j in parts:
        move(came, held, i, j, 0).wait()
        move(held, left, i, j, 1).start()
    for i, j in parts:
        move(held, left, i, j, 1).wait()


def local(tokens, out_grad, gates, expert_ids, w_gate, w_up, w_down):
    lines = lax.axis_size("expert") // ZS
    toks, width = tokens.shape
    depth, ff = w_gate.shape[1:]
    rows = lines * SUB
    any_spec = pl.BlockSpec(memory_space=pl.ANY)
    vmem = pl.BlockSpec(memory_space=pltpu.VMEM)
    dma = pltpu.SemaphoreType.DMA
    grads = jax.ShapeDtypeStruct((1, depth, ff), F32)
    results = pl.pallas_call(
        functools.partial(kernel, lines),
        out_shape=(jax.ShapeDtypeStruct((toks, width), BF16), grads, grads, grads),
        in_specs=[vmem] * 2 + [any_spec] * 5,
        out_specs=(vmem, any_spec, any_spec, any_spec),
        scratch_shapes=[
            pltpu.VMEM((ZS, 16, toks), F32),
            pltpu.VMEM((ZS, toks, width), BF16),
            pltpu.VMEM((ZS, toks, width), BF16),
            pltpu.VMEM((SLOTS_OUT, lines, SUB, width), BF16),
            pltpu.VMEM((SLOTS_OUT, lines, SUB, width), BF16),
            pltpu.VMEM((CHUNKS, lines, SUB, width), BF16),
            pltpu.VMEM((CHUNKS, lines, SUB, width), BF16),
            pltpu.VMEM((3, 2 * depth, ff), BF16),
            pltpu.VMEM((3, 2 * depth, ff), F32),
            pltpu.VMEM((3, depth, ff), F32),
            pltpu.VMEM((ZS, rows, toks), BF16),
            pltpu.VMEM((ZS, rows, toks), BF16),
            pltpu.VMEM((CHUNKS, rows, 1), F32),
            pltpu.VMEM((CHUNKS, lines, SUB, width), BF16),
            pltpu.VMEM((ZS, toks, width), BF16),
            pltpu.VMEM((ZS, toks, width), BF16),
            dma((ZS,)),
            dma((ZS,)),
            dma((2, ZS)),
            dma((2, ZS)),
            dma((2, CHUNKS)),
            dma((2, CHUNKS)),
            dma((CHUNKS,)),
            dma((CHUNKS,)),
            dma((3,)),
            dma((3,)),
            dma((3,)),
            dma((3,)),
            dma((ZS,)),
            dma((ZS,)),
            dma((5,)),
        ],
        compiler_params=pltpu.CompilerParams(
            collective_id=0, has_side_effects=True, vmem_limit_bytes=61 << 20
        ),
        name="experts_backward",
    )(expert_ids.T, gates.T, tokens, out_grad, w_gate, w_up, w_down)
    return pl.pallas_call(
        copies,
        out_shape=tuple(jax.ShapeDtypeStruct(r.shape, r.dtype) for r in results),
        in_specs=[any_spec] * 4,
        out_specs=(any_spec,) * 4,
        scratch_shapes=[pltpu.VMEM(r.shape, r.dtype) for r in results] + [dma((2, 4, PIECES))],
        compiler_params=pltpu.CompilerParams(vmem_limit_bytes=60 << 20),
        name="results",
    )(*results)


def solution(mesh):
    rows = P(("expert", "dp"), None)
    weights = P("expert", "dp", None)
    return jax.shard_map(
        local,
        mesh=mesh,
        in_specs=(rows, rows, rows, rows, weights, weights, weights),
        out_specs=(rows, weights, weights, weights),
        check_vma=False,
    )
```
